128 devices in a mesh: cent: 4 (over y), rows: 32 (over z, x, core).
Axes of the slice: x: 4, y: 4, z: 4, core: 2. Of those that a mesh axis runs over, the one named last changes fastest.
Arguments:
- embeddings: bfloat16 [32768, 2048], P(('cent', 'rows')), may hold values from -6 to 6
- centroids: bfloat16 [16384, 2048], P(('cent', 'rows')), may hold values from -0.125 to 0.125
- cluster: int32 [32768, 1], P(('cent', 'rows')), may hold values from 0 to 127; in each aligned block of 256 rows (0 to 255, 256 to 511, ...) at most 4 rows name the same one
- noise_salt: int32 [1], replicated, may hold values from 0 to 1048575
Outputs:
- perturbed_max: float32 [32768], P(('cent', 'rows'))
- dedup_score: float32 [32768], P(('cent', 'rows'))
- new_centroids: float32 [128, 2048], P(('cent', 'rows'))
The draws below stay inside these ranges and needn't reach their ends.
Inputs may be any that keep to these rules, and one draw needn't show every extreme that they name: In every aligned block of 256 rows (the rows of one device) no cluster is named by more than 4 rows, and in some block some cluster by exactly 4; every cluster is named by some row.
All inputs are finite; a program needn't handle non-finite values.
Results may differ from the reference program's by a relative error of at most 0.0003.
Values may be sent and summed in bfloat16 or wider, within the bound.
A program may use at most 128 MiB of HBM per device.

```python
import math
import jax
import jax.numpy as jnp
import numpy as np
from jax import lax

D = 2048
ROWS_DEV = 256
R = 32768
K = 16384
CLUSTERS = 128
MOST = 4
DEVICES = 128


def level_of(stream_key, dims, cuts, least, largest):
    level, own = 1.0, jax.random.fold_in(stream_key, 6)
    for position, blocks in cuts:
        heights = jnp.exp(jax.random.uniform(jax.random.fold_in(own, position), (blocks,), jnp.float32, least / len(cuts), largest / len(cuts)))
        level = level * jnp.repeat(heights, dims[position] // blocks).reshape([-1 if axis == position else 1 for axis in range(len(dims))])
    return level


def shared_out(rng, own, number, rows, count, top, most, lean):
    sequence = jax.random.permutation(rng, count)
    crowded, common = portions_of(count, rows * top, most, lean, True), portions_of(count, rows * top, most, lean, False)
    places = jnp.arange(count)

    def named(tallies, offset_by):
        used = int((tallies > 0).sum())
        fixed = max(1, used // 4)
        passed = fixed + (places - fixed + offset_by * (used - fixed)) % max(1, count - fixed)
        return jnp.zeros((count,), jnp.int32).at[sequence[jnp.where(places < fixed, places, passed)]].set(jnp.asarray(tallies, jnp.int32))

    tallies = jnp.where(number % 4 == 0, named(crowded, number // 4), named(common, number - number // 4 - 1))
    mixed = jax.random.permutation(jax.random.fold_in(own, 3), count)
    giver, sink = mixed[0:count // 2 * 2:2], mixed[1:count // 2 * 2:2]
    room = jnp.minimum(tallies[giver] - 1, most - tallies[sink]) // 2
    room = jnp.where((giver == sequence[0]) | (sink == sequence[0]) | (tallies[sink] == 0), 0, jnp.maximum(room, 0))
    passed = jax.random.randint(jax.random.fold_in(own, 4), (count // 2,), 0, 1 << 20) % (room + 1)
    tallies = tallies.at[giver].add(-passed).at[sink].add(passed)
    items = jnp.searchsorted(jnp.cumsum(tallies), jnp.arange(rows * top), side="right").astype(jnp.int32)
    table = items.reshape(top, rows).T
    table = table[jax.random.permutation(jax.random.fold_in(own, 1), rows)]
    offset_by = jax.random.randint(jax.random.fold_in(own, 2), (rows, 1), 0, top)
    return jnp.take_along_axis(table, (jnp.arange(top)[None, :] + offset_by) % top, axis=1)


def portions_of(count, total, most, skew, full):
    weights = [(1 << 20) // math.isqrt(standing ** skew) + 1 for standing in range(1, count + 1)]
    largest = most if full else min(most, max(-(-total // count), total * weights[0] // sum(weights)))
    least = 1 if total - largest >= count - 1 else 0
    counts, surplus = [largest] + [least] * (count - 1), total - largest - least * (count - 1)
    while surplus > 0:
        movable = [i for i in range(1, count) if counts[i] < largest] or [i for i in range(1, count) if counts[i] < most]
        whole, budget = sum([weights[i] for i in movable]), surplus
        for i in movable:
            more = min(most - counts[i], max(1, budget * weights[i] // whole), surplus)
            counts[i] = counts[i] + more
            surplus = surplus - more
    return np.array(counts)


def centred(key, extent, scale, limit, shards=(), held_as=jnp.bfloat16):
    values = scale * jax.random.normal(key, extent, jnp.float32)
    if shards:
        values = values * level_of(key, extent, shards, -0.22, 0.18)
    return jnp.clip(values, -limit, limit).astype(held_as)


def setup_inputs(seed: int = 0) -> dict:
    splits = jax.random.split(jax.random.key(seed), 5)
    embeddings = centred(splits[0], (R, D), 1.0, 6.0, ((0, 128),))
    centroids = centred(splits[1], (K, D), D ** -0.5, 0.125, ((0, 128),))
    cluster_keys = jax.random.split(jax.random.fold_in(splits[2], 1), R // ROWS_DEV)
    cluster_turns = jax.random.permutation(jax.random.fold_in(splits[2], 3), R // ROWS_DEV)
    cluster = jax.vmap(lambda own, number: shared_out(jax.random.fold_in(splits[2], 2), own, number, ROWS_DEV, CLUSTERS, 1, MOST, 2))(cluster_keys, cluster_turns).reshape((R, 1))
    noise_salt = jax.random.randint(splits[3], (1,), 0, 1048576).astype(jnp.int32)
    return {"embeddings": embeddings, "centroids": centroids, "cluster": cluster, "noise_salt": noise_salt}


inverse_temp = 3.0
epsilon = 1e-06

def logical_shift(word, amount):
    return lax.shift_right_logical(word, jnp.full(word.shape, amount, jnp.int32))

def gumbel_noise(row_ids, cent_ids, salt_word):
    mixed = (row_ids * 1103515245 + cent_ids * 739982445 + salt_word).astype(jnp.int32)
    mixed = mixed ^ logical_shift(mixed, 16)
    mixed = (mixed * 2146121005).astype(jnp.int32)
    mixed = mixed ^ logical_shift(mixed, 15)
    mixed = (mixed * 1759714725).astype(jnp.int32)
    mixed = mixed ^ logical_shift(mixed, 16)
    low_bits = mixed & 8388607
    uniform = (low_bits.astype(jnp.float32) + 0.5) * (1.0 / 8388608.0)
    return -jnp.log(-jnp.log(uniform))

def cluster_stats(members, valid):
    feature_dim = members.shape[1]
    widened = members.astype(jnp.float32)
    scale = lax.rsqrt(lax.optimization_barrier(jnp.mean(widened * widened, axis=1)) + epsilon)
    gram = lax.dot_general(members, members, (((1,), (1,)), ((), ())), preferred_element_type=jnp.float32)
    similar = gram * scale[:, None] * scale[None, :] * (1.0 / math.sqrt(feature_dim))
    order = jnp.arange(members.shape[0], dtype=jnp.int32)
    usable = valid[None, :] & (order[:, None] != order[None, :])
    highest = lax.optimization_barrier(jnp.max(jnp.where(usable, similar, -1e+30), axis=1))
    scores = jnp.where(jnp.any(usable, axis=1), highest, 0.0)
    total = lax.optimization_barrier(jnp.sum(jnp.where(valid[:, None], widened, 0.0), axis=0))
    center = total * lax.rsqrt(jnp.mean(total * total) + epsilon)
    return (scores, center)

def reference(embeddings, centroids, cluster, noise_salt):
    total_rows = embeddings.shape[0]
    cent_ids = jnp.arange(centroids.shape[0], dtype=jnp.int32)
    block = math.gcd(total_rows, 1024)

    def score_rows(start):
        rows_block = lax.dynamic_slice_in_dim(embeddings, start, block, 0)
        scores = lax.dot_general(rows_block, centroids, (((1,), (1,)), ((), ())), preferred_element_type=jnp.float32)
        row_ids = start + jnp.arange(block, dtype=jnp.int32)
        perturbed = inverse_temp * scores + gumbel_noise(row_ids[:, None], cent_ids[None, :], noise_salt[0])
        return lax.optimization_barrier(jnp.max(perturbed, axis=1))
    starts = jnp.arange(total_rows // block, dtype=jnp.int32) * block
    perturbed_max = lax.map(score_rows, starts).reshape(total_rows)
    assigned = cluster[:, 0].reshape(DEVICES, ROWS_DEV)
    order = jnp.arange(ROWS_DEV, dtype=jnp.int32)
    same = (assigned[:, :, None] == assigned[:, None, :]) & (order[None, None, :] < order[None, :, None])
    rank = lax.optimization_barrier(jnp.sum(same.astype(jnp.int32), axis=2))
    sources = jnp.broadcast_to(jnp.arange(DEVICES, dtype=jnp.int32)[:, None], (DEVICES, ROWS_DEV))
    row_index = jnp.arange(total_rows, dtype=jnp.int32).reshape(DEVICES, ROWS_DEV)
    table = jnp.full((CLUSTERS, DEVICES, MOST), total_rows, jnp.int32).at[assigned, sources, rank].set(row_index)

    def one_cluster(entries):
        valid = entries < total_rows
        members = embeddings[jnp.minimum(entries, total_rows - 1)]
        members = jnp.where(valid[:, None], members, jnp.zeros((), embeddings.dtype))
        return cluster_stats(members, valid)
    scores, centers = lax.map(one_cluster, table.reshape(CLUSTERS, DEVICES * MOST))
    dedup_score = jnp.zeros((total_rows,), jnp.float32).at[table.reshape(-1)].set(scores.reshape(-1), mode='drop')
    return (perturbed_max, dedup_score, centers)
```

```python
import math

import jax
import jax.numpy as jnp
from jax import lax
from jax.sharding import Mesh
from jax.sharding import PartitionSpec as P

inverse_temp = 3.0
epsilon = 1e-06
ALL = ("y", "z", "x", "c")


def logical_shift(word, amount):
    return lax.shift_right_logical(word, jnp.full(word.shape, amount, jnp.int32))


def gumbel_noise(row_ids, cent_ids, salt_word):
    mixed = row_ids * 1103515245 + cent_ids * 739982445 + salt_word
    mixed = mixed ^ logical_shift(mixed, 16)
    mixed = mixed * 2146121005
    mixed = mixed ^ logical_shift(mixed, 15)
    mixed = mixed * 1759714725
    mixed = mixed ^ logical_shift(mixed, 16)
    low_bits = mixed & 8388607
    uniform = (low_bits.astype(jnp.float32) + 0.5) * (1.0 / 8388608.0)
    return -jnp.log(-jnp.log(uniform))


def cluster_stats(members, valid):
    feature_dim = members.shape[1]
    widened = members.astype(jnp.float32)
    scale = lax.rsqrt(jnp.mean(widened * widened, axis=1) + epsilon)
    gram = lax.dot_general(
        members, members, (((1,), (1,)), ((), ())), preferred_element_type=jnp.float32
    )
    similar = gram * scale[:, None] * scale[None, :] * (1.0 / math.sqrt(feature_dim))
    order = jnp.arange(members.shape[0], dtype=jnp.int32)
    usable = valid[None, :] & (order[:, None] != order[None, :])
    highest = jnp.max(jnp.where(usable, similar, -1e30), axis=1)
    scores = jnp.where(jnp.any(usable, axis=1), highest, 0.0)
    total = jnp.sum(jnp.where(valid[:, None], widened, 0.0), axis=0)
    center = total * lax.rsqrt(jnp.mean(total * total) + epsilon)
    return (scores, center)


def shards(embeddings, centroids, cluster, noise_salt):
    rows_dev, feature_dim = embeddings.shape
    cent_dev = centroids.shape[0]
    ny, nz, nx, nc = (lax.axis_size(a) for a in ALL)
    devices = ny * nz * nx * nc
    capacity = max(2, 2 * rows_dev // devices)
    iy, iz, ix, ic = (lax.axis_index(a) for a in ALL)
    me = ((iy * nz + iz) * nx + ix) * nc + ic
    salt_word = noise_salt[0]
    group = lax.all_gather(lax.all_gather(embeddings, "y", axis=0, tiled=True), "c", axis=0, tiled=True)
    piece = lax.all_gather(centroids, ("z", "x"), axis=0, tiled=True)
    position = jnp.arange(nc * ny * rows_dev, dtype=jnp.int32)
    src_c = position // (ny * rows_dev)
    src_y = position // rows_dev % ny
    row_dev = ((src_y * nz + iz) * nx + ix) * nc + src_c
    group_ids = row_dev * rows_dev + position % rows_dev
    cpos = jnp.arange(nz * nx * cent_dev, dtype=jnp.int32)
    cent_dev_ids = ((iy * nz + cpos // (nx * cent_dev)) * nx + cpos // cent_dev % nx) * nc + ic
    cent_ids = cent_dev_ids * cent_dev + cpos % cent_dev
    piece_rows = piece.shape[0]
    block = math.gcd(piece_rows, 512)
    steps = piece_rows // block
    tiles = piece.reshape(steps, block, feature_dim)
    noise = gumbel_noise(group_ids[:, None], cent_ids[None, :], salt_word)
    noise_tiles = noise.reshape(group.shape[0], steps, block).transpose(1, 0, 2)
    initial = jnp.full((group.shape[0],), -1e30, jnp.float32)

    def step(carry, item):
        tile, noise_tile = item
        scores = lax.dot_general(
            group, tile, (((1,), (1,)), ((), ())), preferred_element_type=jnp.float32
        )
        perturbed = inverse_temp * scores + noise_tile
        return (jnp.maximum(carry, jnp.max(perturbed, axis=1)), None)

    result, unused = lax.scan(step, initial, (tiles, noise_tiles))
    merged = lax.pmax(result, ("c", "y"))
    perturbed_max = lax.dynamic_slice_in_dim(merged, (ic * ny + iy) * rows_dev, rows_dev)
    assigned = cluster[:, 0]
    order = jnp.arange(rows_dev, dtype=jnp.int32)
    same = (assigned[:, None] == assigned[None, :]) & (order[None, :] < order[:, None])
    rank = jnp.sum(same.astype(jnp.int32), axis=1)
    slot = assigned * capacity + rank
    outgoing = jnp.zeros((devices * capacity, feature_dim), jnp.bfloat16).at[slot].set(embeddings)
    present = (
        jnp.zeros((devices * capacity,), jnp.bfloat16)
        .at[slot]
        .set(jnp.ones((rows_dev,), jnp.bfloat16))
    )
    received = lax.all_to_all(
        outgoing.reshape(devices, capacity, feature_dim), ALL, split_axis=0, concat_axis=0, tiled=True
    )
    arrived = lax.all_to_all(
        present.reshape(devices, capacity), ALL, split_axis=0, concat_axis=0, tiled=True
    )
    members = received.reshape(devices * capacity, feature_dim)
    valid = arrived.reshape(devices * capacity) > 0.5
    scores, center = cluster_stats(members, valid)
    returned = lax.all_to_all(
        scores.reshape(devices, capacity), ALL, split_axis=0, concat_axis=0, tiled=True
    )
    dedup_score = returned.reshape(devices * capacity)[slot]
    return (perturbed_max, dedup_score, center[None, :])


def solution(mesh):
    cent_count, rows_count = mesh.devices.shape
    cores = 2
    side = math.isqrt(rows_count // cores)
    view = Mesh(mesh.devices.reshape(cent_count, side, rows_count // cores // side, cores), ALL)
    spec = P(ALL, None)
    in_specs = (spec, spec, spec, P())
    out_specs = (P(ALL), P(ALL), spec)
    return jax.shard_map(shards, mesh=view, in_specs=in_specs, out_specs=out_specs, check_vma=False)
```

```python
import math

import jax
import jax.numpy as jnp
from jax import lax
from jax.sharding import Mesh
from jax.sharding import PartitionSpec as P

inverse_temp = 3.0
epsilon = 1e-06
ALL = ("y", "z", "x", "c")


def logical_shift(word, amount):
    return lax.shift_right_logical(word, jnp.full(word.shape, amount, jnp.int32))


def gumbel_noise(row_ids, cent_ids, salt_word):
    mixed = row_ids * 1103515245 + cent_ids * 739982445 + salt_word
    mixed = mixed ^ logical_shift(mixed, 16)
    mixed = mixed * 2146121005
    mixed = mixed ^ logical_shift(mixed, 15)
    mixed = mixed * 1759714725
    mixed = mixed ^ logical_shift(mixed, 16)
    low_bits = mixed & 8388607
    uniform = (low_bits.astype(jnp.float32) + 0.5) * (1.0 / 8388608.0)
    return -jnp.log(-jnp.log(uniform))


def cluster_stats(members, valid):
    feature_dim = members.shape[1]
    widened = members.astype(jnp.float32)
    scale = lax.rsqrt(jnp.mean(widened * widened, axis=1) + epsilon)
    gram = lax.dot_general(
        members, members, (((1,), (1,)), ((), ())), preferred_element_type=jnp.float32
    )
    similar = gram * scale[:, None] * scale[None, :] * (1.0 / math.sqrt(feature_dim))
    order = jnp.arange(members.shape[0], dtype=jnp.int32)
    usable = valid[None, :] & (order[:, None] != order[None, :])
    highest = jnp.max(jnp.where(usable, similar, -1e30), axis=1)
    scores = jnp.where(jnp.any(usable, axis=1), highest, 0.0)
    total = jnp.sum(jnp.where(valid[:, None], widened, 0.0), axis=0)
    center = total * lax.rsqrt(jnp.mean(total * total) + epsilon)
    return (scores, center)


def shards(embeddings, centroids, cluster, noise_salt):
    rows_dev, feature_dim = embeddings.shape
    cent_dev = centroids.shape[0]
    ny, nz, nx, nc = (lax.axis_size(a) for a in ALL)
    devices = ny * nz * nx * nc
    capacity = max(2, 2 * rows_dev // devices)
    iy, iz, ix, ic = (lax.axis_index(a) for a in ALL)
    me = ((iy * nz + iz) * nx + ix) * nc + ic
    salt_word = noise_salt[0]
    ring_y = [
        embeddings if s == 0 else lax.ppermute(embeddings, "y", [(i, (i + s) % ny) for i in range(ny)])
        for s in range(ny)
    ]
    own_rows = jnp.concatenate(ring_y, axis=0)
    other_rows = lax.ppermute(own_rows, "c", [(i, (i + 1) % nc) for i in range(nc)])
    group = jnp.concatenate([own_rows, other_rows], axis=0)
    src_c = jnp.stack([ic, (ic + nc - 1) % nc])
    src_y = (iy - jnp.arange(ny, dtype=jnp.int32)) % ny
    row_dev = ((src_y[None, :] * nz + iz) * nx + ix) * nc + src_c[:, None]
    group_ids = (row_dev[:, :, None] * rows_dev + jnp.arange(rows_dev, dtype=jnp.int32)).reshape(-1)
    shifts = sorted(((dz, dx) for dz in range(nz) for dx in range(nx)),
                    key=lambda d: (min(d[0], nz - d[0]) + min(d[1], nx - d[1]), d))
    pieces = []
    piece_devs = []
    for dz, dx in shifts:
        if dz == 0 and dx == 0:
            pieces.append(centroids)
        else:
            perm = [(z * nx + x, (z + dz) % nz * nx + (x + dx) % nx) for z in range(nz) for x in range(nx)]
            pieces.append(lax.ppermute(centroids, ("z", "x"), perm))
        piece_devs.append(((iy * nz + (iz - dz) % nz) * nx + (ix - dx) % nx) * nc + ic)
    piece_devs = jnp.stack(piece_devs)
    cent_ids = (piece_devs[:, None] * cent_dev + jnp.arange(cent_dev, dtype=jnp.int32)).reshape(-1)
    per_chunk = max(1, 256 // cent_dev)
    noise = gumbel_noise(group_ids[:, None], cent_ids[None, :], salt_word)
    result = None
    for j in range(0, len(pieces), per_chunk):
        tile = jnp.concatenate(pieces[j:j + per_chunk], axis=0)
        scores = lax.dot_general(
            group, tile, (((1,), (1,)), ((), ())), preferred_element_type=jnp.float32
        )
        width = tile.shape[0]
        perturbed = inverse_temp * scores + noise[:, j * cent_dev:j * cent_dev + width]
        part = jnp.max(perturbed, axis=1)
        result = part if result is None else jnp.maximum(result, part)
    blocks = result.reshape(nc, ny, rows_dev)
    best = blocks[0, 0]
    for sc in range(nc):
        for sy in range(ny):
            if sc == 0 and sy == 0:
                continue
            perm = []
            for yy in range(ny):
                for cc in range(nc):
                    dst_y = (yy - sy) % ny
                    dst_c = (cc - sc) % nc
                    perm.append((yy * nc + cc, dst_y * nc + dst_c))
            best = jnp.maximum(best, lax.ppermute(blocks[sc, sy], ("y", "c"), perm))
    perturbed_max = best
    assigned = cluster[:, 0]
    order = jnp.arange(rows_dev, dtype=jnp.int32)
    same = (assigned[:, None] == assigned[None, :]) & (order[None, :] < order[:, None])
    rank = jnp.sum(same.astype(jnp.int32), axis=1)
    slot = assigned * capacity + rank
    outgoing = jnp.zeros((devices * capacity, feature_dim), jnp.bfloat16).at[slot].set(embeddings)
    present = (
        jnp.zeros((devices * capacity,), jnp.bfloat16)
        .at[slot]
        .set(jnp.ones((rows_dev,), jnp.bfloat16))
    )
    received = lax.all_to_all(
        outgoing.reshape(devices, capacity, feature_dim), ALL, split_axis=0, concat_axis=0, tiled=True
    )
    arrived = lax.all_to_all(
        present.reshape(devices, capacity), ALL, split_axis=0, concat_axis=0, tiled=True
    )
    members = received.reshape(devices * capacity, feature_dim)
    valid = arrived.reshape(devices * capacity) > 0.5
    scores, center = cluster_stats(members, valid)
    returned = lax.all_to_all(
        scores.reshape(devices, capacity), ALL, split_axis=0, concat_axis=0, tiled=True
    )
    dedup_score = returned.reshape(devices * capacity)[slot]
    return (perturbed_max, dedup_score, center[None, :])


def solution(mesh):
    cent_count, rows_count = mesh.devices.shape
    cores = 2
    side = math.isqrt(rows_count // cores)
    view = Mesh(mesh.devices.reshape(cent_count, side, rows_count // cores // side, cores), ALL)
    spec = P(ALL, None)
    in_specs = (spec, spec, spec, P())
    out_specs = (P(ALL), P(ALL), spec)
    return jax.shard_map(shards, mesh=view, in_specs=in_specs, out_specs=out_specs, check_vma=False)
```

```python
import functools
import math

import jax
import jax.numpy as jnp
from jax import lax
from jax.experimental import pallas as pl
from jax.experimental.pallas import tpu as pltpu
from jax.sharding import Mesh
from jax.sharding import PartitionSpec as P

inverse_temp = 3.0
epsilon = 1e-06
ALL = ("y", "z", "x", "c")


def logical_shift(word, amount):
    return lax.shift_right_logical(word, jnp.full(word.shape, amount, jnp.int32))


def gumbel_noise(row_ids, cent_ids, salt_word):
    mixed = row_ids * 1103515245 + cent_ids * 739982445 + salt_word
    mixed = mixed ^ logical_shift(mixed, 16)
    mixed = mixed * 2146121005
    mixed = mixed ^ logical_shift(mixed, 15)
    mixed = mixed * 1759714725
    mixed = mixed ^ logical_shift(mixed, 16)
    low_bits = mixed & 8388607
    uniform = (low_bits.astype(jnp.float32) + 0.5) * (1.0 / 8388608.0)
    return -jnp.log(-jnp.log(uniform))


def gather_kernel(axes, sizes, x_ref, out_ref, send_sem, recv_sem, local_sem):
    n = math.prod(sizes)
    where = {a: lax.axis_index(a) for a in ALL}
    me = 0
    for a, size in zip(axes, sizes):
        me = me * size + where[a]

    def device_of(index):
        coords = dict(where)
        for a, size in reversed(list(zip(axes, sizes))):
            coords[a] = lax.rem(index, size)
            index = index // size
        return tuple(coords[a] for a in ALL)

    peers = [lax.rem(me + k, n) for k in range(n)]
    barrier = pltpu.get_barrier_semaphore()
    for k in range(1, n):
        pl.semaphore_signal(barrier, inc=1, device_id=device_of(peers[k]), device_id_type=pl.DeviceIdType.MESH)
    pl.semaphore_wait(barrier, n - 1)
    local = pltpu.make_async_copy(x_ref, out_ref.at[me], local_sem)
    local.start()
    sends = []
    for k in range(1, n):
        copy = pltpu.make_async_remote_copy(
            src_ref=x_ref,
            dst_ref=out_ref.at[me],
            send_sem=send_sem.at[k],
            recv_sem=recv_sem.at[me],
            device_id=device_of(peers[k]),
            device_id_type=pl.DeviceIdType.MESH,
        )
        copy.start()
        sends.append(copy)
    for k in range(1, n):
        source = lax.rem(me + n - k, n)
        pltpu.make_async_remote_copy(
            src_ref=x_ref,
            dst_ref=out_ref.at[source],
            send_sem=send_sem.at[k],
            recv_sem=recv_sem.at[source],
            device_id=device_of(source),
            device_id_type=pl.DeviceIdType.MESH,
        ).wait_recv()
    for copy in sends:
        copy.wait_send()
    local.wait()


def gather(x, axes, collective_id):
    sizes = tuple(lax.axis_size(a) for a in axes)
    n = math.prod(sizes)
    out = pl.pallas_call(
        functools.partial(gather_kernel, axes, sizes),
        out_shape=jax.ShapeDtypeStruct((n,) + x.shape, x.dtype),
        in_specs=[pl.BlockSpec(memory_space=pl.ANY)],
        out_specs=pl.BlockSpec(memory_space=pl.ANY),
        scratch_shapes=[
            pltpu.SemaphoreType.DMA((n,)),
            pltpu.SemaphoreType.DMA((n,)),
            pltpu.SemaphoreType.DMA,
        ],
        compiler_params=pltpu.CompilerParams(collective_id=collective_id, has_side_effects=True),
    )(x)
    return out.reshape((n * x.shape[0],) + x.shape[1:])


def cluster_stats(members, valid):
    feature_dim = members.shape[1]
    widened = members.astype(jnp.float32)
    scale = lax.rsqrt(jnp.mean(widened * widened, axis=1) + epsilon)
    gram = lax.dot_general(
        members, members, (((1,), (1,)), ((), ())), preferred_element_type=jnp.float32
    )
    similar = gram * scale[:, None] * scale[None, :] * (1.0 / math.sqrt(feature_dim))
    order = jnp.arange(members.shape[0], dtype=jnp.int32)
    usable = valid[None, :] & (order[:, None] != order[None, :])
    highest = jnp.max(jnp.where(usable, similar, -1e30), axis=1)
    scores = jnp.where(jnp.any(usable, axis=1), highest, 0.0)
    total = jnp.sum(jnp.where(valid[:, None], widened, 0.0), axis=0)
    center = total * lax.rsqrt(jnp.mean(total * total) + epsilon)
    return (scores, center)


def shards(embeddings, centroids, cluster, noise_salt):
    rows_dev, feature_dim = embeddings.shape
    cent_dev = centroids.shape[0]
    ny, nz, nx, nc = (lax.axis_size(a) for a in ALL)
    devices = ny * nz * nx * nc
    capacity = max(2, 2 * rows_dev // devices)
    iy, iz, ix, ic = (lax.axis_index(a) for a in ALL)
    me = ((iy * nz + iz) * nx + ix) * nc + ic
    salt_word = noise_salt[0]
    group = gather(gather(embeddings, ("y",), 0), ("c",), 1)
    piece = gather(centroids, ("z", "x"), 2)
    position = jnp.arange(nc * ny * rows_dev, dtype=jnp.int32)
    src_c = position // (ny * rows_dev)
    src_y = position // rows_dev % ny
    row_dev = ((src_y * nz + iz) * nx + ix) * nc + src_c
    group_ids = row_dev * rows_dev + position % rows_dev
    cpos = jnp.arange(nz * nx * cent_dev, dtype=jnp.int32)
    cent_dev_ids = ((iy * nz + cpos // (nx * cent_dev)) * nx + cpos // cent_dev % nx) * nc + ic
    cent_ids = cent_dev_ids * cent_dev + cpos % cent_dev
    piece_rows = piece.shape[0]
    block = math.gcd(piece_rows, 512)
    steps = piece_rows // block
    tiles = piece.reshape(steps, block, feature_dim)
    noise = gumbel_noise(group_ids[:, None], cent_ids[None, :], salt_word)
    noise_tiles = noise.reshape(group.shape[0], steps, block).transpose(1, 0, 2)
    initial = jnp.full((group.shape[0],), -1e30, jnp.float32)

    def step(carry, item):
        tile, noise_tile = item
        scores = lax.dot_general(
            group, tile, (((1,), (1,)), ((), ())), preferred_element_type=jnp.float32
        )
        perturbed = inverse_temp * scores + noise_tile
        return (jnp.maximum(carry, jnp.max(perturbed, axis=1)), None)

    result, unused = lax.scan(step, initial, (tiles, noise_tiles))
    merged = lax.pmax(result, ("c", "y"))
    perturbed_max = lax.dynamic_slice_in_dim(merged, (ic * ny + iy) * rows_dev, rows_dev)
    assigned = cluster[:, 0]
    order = jnp.arange(rows_dev, dtype=jnp.int32)
    same = (assigned[:, None] == assigned[None, :]) & (order[None, :] < order[:, None])
    rank = jnp.sum(same.astype(jnp.int32), axis=1)
    slot = assigned * capacity + rank
    outgoing = jnp.zeros((devices * capacity, feature_dim), jnp.bfloat16).at[slot].set(embeddings)
    present = (
        jnp.zeros((devices * capacity,), jnp.bfloat16)
        .at[slot]
        .set(jnp.ones((rows_dev,), jnp.bfloat16))
    )
    received = lax.all_to_all(
        outgoing.reshape(devices, capacity, feature_dim), ALL, split_axis=0, concat_axis=0, tiled=True
    )
    arrived = lax.all_to_all(
        present.reshape(devices, capacity), ALL, split_axis=0, concat_axis=0, tiled=True
    )
    members = received.reshape(devices * capacity, feature_dim)
    valid = arrived.reshape(devices * capacity) > 0.5
    scores, center = cluster_stats(members, valid)
    returned = lax.all_to_all(
        scores.reshape(devices, capacity), ALL, split_axis=0, concat_axis=0, tiled=True
    )
    dedup_score = returned.reshape(devices * capacity)[slot]
    return (perturbed_max, dedup_score, center[None, :])


def solution(mesh):
    cent_count, rows_count = mesh.devices.shape
    cores = 2
    side = math.isqrt(rows_count // cores)
    view = Mesh(mesh.devices.reshape(cent_count, side, rows_count // cores // side, cores), ALL)
    spec = P(ALL, None)
    in_specs = (spec, spec, spec, P())
    out_specs = (P(ALL), P(ALL), spec)
    return jax.shard_map(shards, mesh=view, in_specs=in_specs, out_specs=out_specs, check_vma=False)
```

```python
import functools
import math

import jax
import jax.numpy as jnp
from jax import lax
from jax.experimental import pallas as pl
from jax.experimental.pallas import tpu as pltpu
from jax.sharding import Mesh
from jax.sharding import PartitionSpec as P

inverse_temp = 3.0
epsilon = 1e-06
ALL = ("y", "z", "x", "c")


def logical_shift(word, amount):
    return lax.shift_right_logical(word, jnp.full(word.shape, amount, jnp.int32))


def gumbel_noise(row_ids, cent_ids, salt_word):
    mixed = row_ids * 1103515245 + cent_ids * 739982445 + salt_word
    mixed = mixed ^ logical_shift(mixed, 16)
    mixed = mixed * 2146121005
    mixed = mixed ^ logical_shift(mixed, 15)
    mixed = mixed * 1759714725
    mixed = mixed ^ logical_shift(mixed, 16)
    low_bits = mixed & 8388607
    uniform = (low_bits.astype(jnp.float32) + 0.5) * (1.0 / 8388608.0)
    return -jnp.log(-jnp.log(uniform))


def gather_kernel(axes, sizes, x_ref, out_ref, send_sem, recv_sem, local_sem):
    n = math.prod(sizes)
    where = {a: lax.axis_index(a) for a in ALL}
    me = 0
    for a, size in zip(axes, sizes):
        me = me * size + where[a]

    def device_of(index):
        coords = dict(where)
        for a, size in reversed(list(zip(axes, sizes))):
            coords[a] = lax.rem(index, size)
            index = index // size
        return tuple(coords[a] for a in ALL)

    peers = [lax.rem(me + k, n) for k in range(n)]
    barrier = pltpu.get_barrier_semaphore()
    for k in range(1, n):
        pl.semaphore_signal(barrier, inc=1, device_id=device_of(peers[k]), device_id_type=pl.DeviceIdType.MESH)
    pl.semaphore_wait(barrier, n - 1)
    local = pltpu.make_async_copy(x_ref, out_ref.at[me], local_sem)
    local.start()
    sends = []
    for k in range(1, n):
        copy = pltpu.make_async_remote_copy(
            src_ref=x_ref,
            dst_ref=out_ref.at[me],
            send_sem=send_sem.at[k],
            recv_sem=recv_sem.at[me],
            device_id=device_of(peers[k]),
            device_id_type=pl.DeviceIdType.MESH,
        )
        copy.start()
        sends.append(copy)
    for k in range(1, n):
        source = lax.rem(me + n - k, n)
        pltpu.make_async_remote_copy(
            src_ref=x_ref,
            dst_ref=out_ref.at[source],
            send_sem=send_sem.at[k],
            recv_sem=recv_sem.at[source],
            device_id=device_of(source),
            device_id_type=pl.DeviceIdType.MESH,
        ).wait_recv()
    for copy in sends:
        copy.wait_send()
    local.wait()


def gather(x, axes, collective_id):
    sizes = tuple(lax.axis_size(a) for a in axes)
    n = math.prod(sizes)
    out = pl.pallas_call(
        functools.partial(gather_kernel, axes, sizes),
        out_shape=jax.ShapeDtypeStruct((n,) + x.shape, x.dtype),
        in_specs=[pl.BlockSpec(memory_space=pl.ANY)],
        out_specs=pl.BlockSpec(memory_space=pl.ANY),
        scratch_shapes=[
            pltpu.SemaphoreType.DMA((n,)),
            pltpu.SemaphoreType.DMA((n,)),
            pltpu.SemaphoreType.DMA,
        ],
        compiler_params=pltpu.CompilerParams(collective_id=collective_id, has_side_effects=True),
    )(x)
    return out.reshape((n * x.shape[0],) + x.shape[1:])


def cluster_stats(members, valid):
    feature_dim = members.shape[1]
    widened = members.astype(jnp.float32)
    scale = lax.rsqrt(jnp.mean(widened * widened, axis=1) + epsilon)
    gram = lax.dot_general(
        members, members, (((1,), (1,)), ((), ())), preferred_element_type=jnp.float32
    )
    similar = gram * scale[:, None] * scale[None, :] * (1.0 / math.sqrt(feature_dim))
    order = jnp.arange(members.shape[0], dtype=jnp.int32)
    usable = valid[None, :] & (order[:, None] != order[None, :])
    highest = jnp.max(jnp.where(usable, similar, -1e30), axis=1)
    scores = jnp.where(jnp.any(usable, axis=1), highest, 0.0)
    total = jnp.sum(jnp.where(valid[:, None], widened, 0.0), axis=0)
    center = total * lax.rsqrt(jnp.mean(total * total) + epsilon)
    return (scores, center)


def shards(embeddings, centroids, cluster, noise_salt):
    rows_dev, feature_dim = embeddings.shape
    cent_dev = centroids.shape[0]
    ny, nz, nx, nc = (lax.axis_size(a) for a in ALL)
    devices = ny * nz * nx * nc
    capacity = max(2, 2 * rows_dev // devices)
    iy, iz, ix, ic = (lax.axis_index(a) for a in ALL)
    me = ((iy * nz + iz) * nx + ix) * nc + ic
    salt_word = noise_salt[0]
    own_rows = gather(embeddings, ("y",), 0)
    other_rows = lax.ppermute(own_rows, "c", [(i, (i + 1) % nc) for i in range(nc)])
    group = jnp.concatenate([own_rows, other_rows], axis=0)
    piece = lax.all_gather(centroids, ("z", "x"), axis=0, tiled=True)
    src_c = jnp.stack([ic, (ic + nc - 1) % nc])
    src_y = jnp.arange(ny, dtype=jnp.int32)
    row_dev = ((src_y[None, :] * nz + iz) * nx + ix) * nc + src_c[:, None]
    group_ids = (row_dev[:, :, None] * rows_dev + jnp.arange(rows_dev, dtype=jnp.int32)).reshape(-1)
    cpos = jnp.arange(nz * nx * cent_dev, dtype=jnp.int32)
    cent_dev_ids = ((iy * nz + cpos // (nx * cent_dev)) * nx + cpos // cent_dev % nx) * nc + ic
    cent_ids = cent_dev_ids * cent_dev + cpos % cent_dev
    piece_rows = piece.shape[0]
    block = math.gcd(piece_rows, 512)
    steps = piece_rows // block
    tiles = piece.reshape(steps, block, feature_dim)
    noise = gumbel_noise(group_ids[:, None], cent_ids[None, :], salt_word)
    noise_tiles = noise.reshape(group.shape[0], steps, block).transpose(1, 0, 2)
    initial = jnp.full((group.shape[0],), -1e30, jnp.float32)

    def step(carry, item):
        tile, noise_tile = item
        scores = lax.dot_general(
            group, tile, (((1,), (1,)), ((), ())), preferred_element_type=jnp.float32
        )
        perturbed = inverse_temp * scores + noise_tile
        return (jnp.maximum(carry, jnp.max(perturbed, axis=1)), None)

    result, unused = lax.scan(step, initial, (tiles, noise_tiles))
    result = jnp.roll(result, ic * (ny * rows_dev))
    merged = lax.pmax(result, ("c", "y"))
    perturbed_max = lax.dynamic_slice_in_dim(merged, (ic * ny + iy) * rows_dev, rows_dev)
    assigned = cluster[:, 0]
    order = jnp.arange(rows_dev, dtype=jnp.int32)
    same = (assigned[:, None] == assigned[None, :]) & (order[None, :] < order[:, None])
    rank = jnp.sum(same.astype(jnp.int32), axis=1)
    slot = assigned * capacity + rank
    outgoing = jnp.zeros((devices * capacity, feature_dim), jnp.bfloat16).at[slot].set(embeddings)
    present = (
        jnp.zeros((devices * capacity,), jnp.bfloat16)
        .at[slot]
        .set(jnp.ones((rows_dev,), jnp.bfloat16))
    )
    received = lax.all_to_all(
        outgoing.reshape(devices, capacity, feature_dim), ALL, split_axis=0, concat_axis=0, tiled=True
    )
    arrived = lax.all_to_all(
        present.reshape(devices, capacity), ALL, split_axis=0, concat_axis=0, tiled=True
    )
    members = received.reshape(devices * capacity, feature_dim)
    valid = arrived.reshape(devices * capacity) > 0.5
    scores, center = cluster_stats(members, valid)
    returned = lax.all_to_all(
        scores.reshape(devices, capacity), ALL, split_axis=0, concat_axis=0, tiled=True
    )
    dedup_score = returned.reshape(devices * capacity)[slot]
    return (perturbed_max, dedup_score, center[None, :])


def solution(mesh):
    cent_count, rows_count = mesh.devices.shape
    cores = 2
    side = math.isqrt(rows_count // cores)
    view = Mesh(mesh.devices.reshape(cent_count, side, rows_count // cores // side, cores), ALL)
    spec = P(ALL, None)
    in_specs = (spec, spec, spec, P())
    out_specs = (P(ALL), P(ALL), spec)
    return jax.shard_map(shards, mesh=view, in_specs=in_specs, out_specs=out_specs, check_vma=False)
```

```python
import functools
import math

import jax
import jax.numpy as jnp
from jax import lax
from jax.experimental import pallas as pl
from jax.experimental.pallas import tpu as pltpu
from jax.sharding import Mesh
from jax.sharding import PartitionSpec as P

inverse_temp = 3.0
epsilon = 1e-06
ALL = ("y", "z", "x", "c")


def logical_shift(word, amount):
    return lax.shift_right_logical(word, jnp.full(word.shape, amount, jnp.int32))


def gumbel_noise(row_ids, cent_ids, salt_word):
    mixed = row_ids * 1103515245 + cent_ids * 739982445 + salt_word
    mixed = mixed ^ logical_shift(mixed, 16)
    mixed = mixed * 2146121005
    mixed = mixed ^ logical_shift(mixed, 15)
    mixed = mixed * 1759714725
    mixed = mixed ^ logical_shift(mixed, 16)
    low_bits = mixed & 8388607
    uniform = (low_bits.astype(jnp.float32) + 0.5) * (1.0 / 8388608.0)
    return -jnp.log(-jnp.log(uniform))


def gather_kernel(axes, sizes, x_ref, out_ref, send_sem, recv_sem, local_sem):
    n = math.prod(sizes)
    where = {a: lax.axis_index(a) for a in ALL}
    me = 0
    for a, size in zip(axes, sizes):
        me = me * size + where[a]

    def device_of(index):
        coords = dict(where)
        for a, size in reversed(list(zip(axes, sizes))):
            coords[a] = lax.rem(index, size)
            index = index // size
        return tuple(coords[a] for a in ALL)

    peers = [lax.rem(me + k, n) for k in range(n)]
    barrier = pltpu.get_barrier_semaphore()
    for k in range(1, n):
        pl.semaphore_signal(barrier, inc=1, device_id=device_of(peers[k]), device_id_type=pl.DeviceIdType.MESH)
    pl.semaphore_wait(barrier, n - 1)
    local = pltpu.make_async_copy(x_ref, out_ref.at[me], local_sem)
    local.start()
    sends = []
    for k in range(1, n):
        copy = pltpu.make_async_remote_copy(
            src_ref=x_ref,
            dst_ref=out_ref.at[me],
            send_sem=send_sem.at[k],
            recv_sem=recv_sem.at[me],
            device_id=device_of(peers[k]),
            device_id_type=pl.DeviceIdType.MESH,
        )
        copy.start()
        sends.append(copy)
    for k in range(1, n):
        source = lax.rem(me + n - k, n)
        pltpu.make_async_remote_copy(
            src_ref=x_ref,
            dst_ref=out_ref.at[source],
            send_sem=send_sem.at[k],
            recv_sem=recv_sem.at[source],
            device_id=device_of(source),
            device_id_type=pl.DeviceIdType.MESH,
        ).wait_recv()
    for copy in sends:
        copy.wait_send()
    local.wait()


def gather(x, axes, collective_id):
    sizes = tuple(lax.axis_size(a) for a in axes)
    n = math.prod(sizes)
    out = pl.pallas_call(
        functools.partial(gather_kernel, axes, sizes),
        out_shape=jax.ShapeDtypeStruct((n,) + x.shape, x.dtype),
        in_specs=[pl.BlockSpec(memory_space=pl.ANY)],
        out_specs=pl.BlockSpec(memory_space=pl.ANY),
        scratch_shapes=[
            pltpu.SemaphoreType.DMA((n,)),
            pltpu.SemaphoreType.DMA((n,)),
            pltpu.SemaphoreType.DMA,
        ],
        compiler_params=pltpu.CompilerParams(collective_id=collective_id, has_side_effects=True),
    )(x)
    return out.reshape((n * x.shape[0],) + x.shape[1:])


def cluster_stats(members, valid):
    feature_dim = members.shape[1]
    widened = members.astype(jnp.float32)
    scale = lax.rsqrt(jnp.mean(widened * widened, axis=1) + epsilon)
    gram = lax.dot_general(
        members, members, (((1,), (1,)), ((), ())), preferred_element_type=jnp.float32
    )
    similar = gram * scale[:, None] * scale[None, :] * (1.0 / math.sqrt(feature_dim))
    order = jnp.arange(members.shape[0], dtype=jnp.int32)
    usable = valid[None, :] & (order[:, None] != order[None, :])
    highest = jnp.max(jnp.where(usable, similar, -1e30), axis=1)
    scores = jnp.where(jnp.any(usable, axis=1), highest, 0.0)
    total = jnp.sum(jnp.where(valid[:, None], widened, 0.0), axis=0)
    center = total * lax.rsqrt(jnp.mean(total * total) + epsilon)
    return (scores, center)


def shards(embeddings, centroids, cluster, noise_salt):
    rows_dev, feature_dim = embeddings.shape
    cent_dev = centroids.shape[0]
    ny, nz, nx, nc = (lax.axis_size(a) for a in ALL)
    devices = ny * nz * nx * nc
    capacity = max(2, 2 * rows_dev // devices)
    iy, iz, ix, ic = (lax.axis_index(a) for a in ALL)
    me = ((iy * nz + iz) * nx + ix) * nc + ic
    salt_word = noise_salt[0]
    swap = [(i, (i + 1) % nc) for i in range(nc)]
    ring_y = [
        embeddings if s == 0 else lax.ppermute(embeddings, "y", [(i, (i + s) % ny) for i in range(ny)])
        for s in range(ny)
    ]
    group = jnp.concatenate(ring_y + [lax.ppermute(p, "c", swap) for p in ring_y], axis=0)
    piece = lax.all_gather(centroids, ("z", "x"), axis=0, tiled=True)
    src_c = jnp.stack([ic, (ic + nc - 1) % nc])
    src_y = (iy - jnp.arange(ny, dtype=jnp.int32)) % ny
    row_dev = ((src_y[None, :] * nz + iz) * nx + ix) * nc + src_c[:, None]
    group_ids = (row_dev[:, :, None] * rows_dev + jnp.arange(rows_dev, dtype=jnp.int32)).reshape(-1)
    canonical = ((src_c[:, None] * ny + src_y[None, :])[:, :, None] * rows_dev
                 + jnp.arange(rows_dev, dtype=jnp.int32)).reshape(-1)
    cpos = jnp.arange(nz * nx * cent_dev, dtype=jnp.int32)
    cent_dev_ids = ((iy * nz + cpos // (nx * cent_dev)) * nx + cpos // cent_dev % nx) * nc + ic
    cent_ids = cent_dev_ids * cent_dev + cpos % cent_dev
    piece_rows = piece.shape[0]
    block = math.gcd(piece_rows, 512)
    steps = piece_rows // block
    tiles = piece.reshape(steps, block, feature_dim)
    noise = gumbel_noise(group_ids[:, None], cent_ids[None, :], salt_word)
    noise_tiles = noise.reshape(group.shape[0], steps, block).transpose(1, 0, 2)
    initial = jnp.full((group.shape[0],), -1e30, jnp.float32)

    def step(carry, item):
        tile, noise_tile = item
        scores = lax.dot_general(
            group, tile, (((1,), (1,)), ((), ())), preferred_element_type=jnp.float32
        )
        perturbed = inverse_temp * scores + noise_tile
        return (jnp.maximum(carry, jnp.max(perturbed, axis=1)), None)

    result, unused = lax.scan(step, initial, (tiles, noise_tiles))
    result = jnp.zeros_like(result).at[canonical].set(result, unique_indices=True)
    merged = lax.pmax(result, ("c", "y"))
    perturbed_max = lax.dynamic_slice_in_dim(merged, (ic * ny + iy) * rows_dev, rows_dev)
    assigned = cluster[:, 0]
    order = jnp.arange(rows_dev, dtype=jnp.int32)
    same = (assigned[:, None] == assigned[None, :]) & (order[None, :] < order[:, None])
    rank = jnp.sum(same.astype(jnp.int32), axis=1)
    slot = assigned * capacity + rank
    outgoing = jnp.zeros((devices * capacity, feature_dim), jnp.bfloat16).at[slot].set(embeddings)
    present = (
        jnp.zeros((devices * capacity,), jnp.bfloat16)
        .at[slot]
        .set(jnp.ones((rows_dev,), jnp.bfloat16))
    )
    received = lax.all_to_all(
        outgoing.reshape(devices, capacity, feature_dim), ALL, split_axis=0, concat_axis=0, tiled=True
    )
    arrived = lax.all_to_all(
        present.reshape(devices, capacity), ALL, split_axis=0, concat_axis=0, tiled=True
    )
    members = received.reshape(devices * capacity, feature_dim)
    valid = arrived.reshape(devices * capacity) > 0.5
    scores, center = cluster_stats(members, valid)
    returned = lax.all_to_all(
        scores.reshape(devices, capacity), ALL, split_axis=0, concat_axis=0, tiled=True
    )
    dedup_score = returned.reshape(devices * capacity)[slot]
    return (perturbed_max, dedup_score, center[None, :])


def solution(mesh):
    cent_count, rows_count = mesh.devices.shape
    cores = 2
    side = math.isqrt(rows_count // cores)
    view = Mesh(mesh.devices.reshape(cent_count, side, rows_count // cores // side, cores), ALL)
    spec = P(ALL, None)
    in_specs = (spec, spec, spec, P())
    out_specs = (P(ALL), P(ALL), spec)
    return jax.shard_map(shards, mesh=view, in_specs=in_specs, out_specs=out_specs, check_vma=False)
```

```python
import functools
import math

import jax
import jax.numpy as jnp
from jax import lax
from jax.experimental import pallas as pl
from jax.experimental.pallas import tpu as pltpu
from jax.sharding import Mesh
from jax.sharding import PartitionSpec as P

inverse_temp = 3.0
epsilon = 1e-06
ALL = ("y", "z", "x", "c")


def logical_shift(word, amount):
    return lax.shift_right_logical(word, jnp.full(word.shape, amount, jnp.int32))


def gumbel_noise(row_ids, cent_ids, salt_word):
    mixed = row_ids * 1103515245 + cent_ids * 739982445 + salt_word
    mixed = mixed ^ logical_shift(mixed, 16)
    mixed = mixed * 2146121005
    mixed = mixed ^ logical_shift(mixed, 15)
    mixed = mixed * 1759714725
    mixed = mixed ^ logical_shift(mixed, 16)
    low_bits = mixed & 8388607
    uniform = (low_bits.astype(jnp.float32) + 0.5) * (1.0 / 8388608.0)
    return -jnp.log(-jnp.log(uniform))


def gather_kernel(axes, sizes, x_ref, out_ref, send_sem, recv_sem, local_sem):
    n = math.prod(sizes)
    where = {a: lax.axis_index(a) for a in ALL}
    me = 0
    for a, size in zip(axes, sizes):
        me = me * size + where[a]

    def device_of(index):
        coords = dict(where)
        for a, size in reversed(list(zip(axes, sizes))):
            coords[a] = lax.rem(index, size)
            index = index // size
        return tuple(coords[a] for a in ALL)

    peers = [lax.rem(me + k, n) for k in range(n)]
    barrier = pltpu.get_barrier_semaphore()
    for k in range(1, n):
        pl.semaphore_signal(barrier, inc=1, device_id=device_of(peers[k]), device_id_type=pl.DeviceIdType.MESH)
    pl.semaphore_wait(barrier, n - 1)
    local = pltpu.make_async_copy(x_ref, out_ref.at[me], local_sem)
    local.start()
    sends = []
    for k in range(1, n):
        copy = pltpu.make_async_remote_copy(
            src_ref=x_ref,
            dst_ref=out_ref.at[me],
            send_sem=send_sem.at[k],
            recv_sem=recv_sem.at[me],
            device_id=device_of(peers[k]),
            device_id_type=pl.DeviceIdType.MESH,
        )
        copy.start()
        sends.append(copy)
    for k in range(1, n):
        source = lax.rem(me + n - k, n)
        pltpu.make_async_remote_copy(
            src_ref=x_ref,
            dst_ref=out_ref.at[source],
            send_sem=send_sem.at[k],
            recv_sem=recv_sem.at[source],
            device_id=device_of(source),
            device_id_type=pl.DeviceIdType.MESH,
        ).wait_recv()
    for copy in sends:
        copy.wait_send()
    local.wait()


def gather(x, axes, collective_id):
    sizes = tuple(lax.axis_size(a) for a in axes)
    n = math.prod(sizes)
    out = pl.pallas_call(
        functools.partial(gather_kernel, axes, sizes),
        out_shape=jax.ShapeDtypeStruct((n,) + x.shape, x.dtype),
        in_specs=[pl.BlockSpec(memory_space=pl.ANY)],
        out_specs=pl.BlockSpec(memory_space=pl.ANY),
        scratch_shapes=[
            pltpu.SemaphoreType.DMA((n,)),
            pltpu.SemaphoreType.DMA((n,)),
            pltpu.SemaphoreType.DMA,
        ],
        compiler_params=pltpu.CompilerParams(collective_id=collective_id, has_side_effects=True),
    )(x)
    return out.reshape((n * x.shape[0],) + x.shape[1:])


def cluster_stats(members, valid):
    feature_dim = members.shape[1]
    widened = members.astype(jnp.float32)
    scale = lax.rsqrt(jnp.mean(widened * widened, axis=1) + epsilon)
    gram = lax.dot_general(
        members, members, (((1,), (1,)), ((), ())), preferred_element_type=jnp.float32
    )
    similar = gram * scale[:, None] * scale[None, :] * (1.0 / math.sqrt(feature_dim))
    order = jnp.arange(members.shape[0], dtype=jnp.int32)
    usable = valid[None, :] & (order[:, None] != order[None, :])
    highest = jnp.max(jnp.where(usable, similar, -1e30), axis=1)
    scores = jnp.where(jnp.any(usable, axis=1), highest, 0.0)
    total = jnp.sum(jnp.where(valid[:, None], widened, 0.0), axis=0)
    center = total * lax.rsqrt(jnp.mean(total * total) + epsilon)
    return (scores, center)


def shards(embeddings, centroids, cluster, noise_salt):
    rows_dev, feature_dim = embeddings.shape
    cent_dev = centroids.shape[0]
    ny, nz, nx, nc = (lax.axis_size(a) for a in ALL)
    devices = ny * nz * nx * nc
    capacity = max(2, 2 * rows_dev // devices)
    iy, iz, ix, ic = (lax.axis_index(a) for a in ALL)
    me = ((iy * nz + iz) * nx + ix) * nc + ic
    salt_word = noise_salt[0]
    swap = [(i, (i + 1) % nc) for i in range(nc)]
    ring_y = [
        embeddings if s == 0 else lax.ppermute(embeddings, "y", [(i, (i + s) % ny) for i in range(ny)])
        for s in range(ny)
    ]
    group = jnp.concatenate(ring_y + [lax.ppermute(p, "c", swap) for p in ring_y], axis=0)
    piece = lax.all_gather(centroids, ("z", "x"), axis=0, tiled=True)
    src_c = jnp.stack([ic, (ic + nc - 1) % nc])
    src_y = (iy - jnp.arange(ny, dtype=jnp.int32)) % ny
    row_dev = ((src_y[None, :] * nz + iz) * nx + ix) * nc + src_c[:, None]
    group_ids = (row_dev[:, :, None] * rows_dev + jnp.arange(rows_dev, dtype=jnp.int32)).reshape(-1)
    cpos = jnp.arange(nz * nx * cent_dev, dtype=jnp.int32)
    cent_dev_ids = ((iy * nz + cpos // (nx * cent_dev)) * nx + cpos // cent_dev % nx) * nc + ic
    cent_ids = cent_dev_ids * cent_dev + cpos % cent_dev
    piece_rows = piece.shape[0]
    block = math.gcd(piece_rows, 512)
    steps = piece_rows // block
    tiles = piece.reshape(steps, block, feature_dim)
    noise = gumbel_noise(group_ids[:, None], cent_ids[None, :], salt_word)
    noise_tiles = noise.reshape(group.shape[0], steps, block).transpose(1, 0, 2)
    initial = jnp.full((group.shape[0],), -1e30, jnp.float32)

    def step(carry, item):
        tile, noise_tile = item
        scores = lax.dot_general(
            group, tile, (((1,), (1,)), ((), ())), preferred_element_type=jnp.float32
        )
        perturbed = inverse_temp * scores + noise_tile
        return (jnp.maximum(carry, jnp.max(perturbed, axis=1)), None)

    result, unused = lax.scan(step, initial, (tiles, noise_tiles))
    blocks = result.reshape(nc, ny, rows_dev)
    best = blocks[0, 0]
    for sc in range(nc):
        for sy in range(ny):
            if sc == 0 and sy == 0:
                continue
            perm = [(yy * nc + cc, (yy - sy) % ny * nc + (cc - sc) % nc) for yy in range(ny) for cc in range(nc)]
            best = jnp.maximum(best, lax.ppermute(blocks[sc, sy], ("y", "c"), perm))
    perturbed_max = best
    assigned = cluster[:, 0]
    order = jnp.arange(rows_dev, dtype=jnp.int32)
    same = (assigned[:, None] == assigned[None, :]) & (order[None, :] < order[:, None])
    rank = jnp.sum(same.astype(jnp.int32), axis=1)
    slot = assigned * capacity + rank
    flag_width = 128
    tagged = jnp.concatenate([embeddings, jnp.ones((rows_dev, flag_width), jnp.bfloat16)], axis=1)
    outgoing = jnp.zeros((devices * capacity, feature_dim + flag_width), jnp.bfloat16).at[slot].set(tagged)
    received = lax.all_to_all(
        outgoing.reshape(devices, capacity, feature_dim + flag_width), ALL, split_axis=0, concat_axis=0, tiled=True
    ).reshape(devices * capacity, feature_dim + flag_width)
    members = received[:, :feature_dim]
    valid = received[:, feature_dim] > 0.5
    scores, center = cluster_stats(members, valid)
    returned = lax.all_to_all(
        scores.reshape(devices, capacity), ALL, split_axis=0, concat_axis=0, tiled=True
    )
    dedup_score = returned.reshape(devices * capacity)[slot]
    return (perturbed_max, dedup_score, center[None, :])


def solution(mesh):
    cent_count, rows_count = mesh.devices.shape
    cores = 2
    side = math.isqrt(rows_count // cores)
    view = Mesh(mesh.devices.reshape(cent_count, side, rows_count // cores // side, cores), ALL)
    spec = P(ALL, None)
    in_specs = (spec, spec, spec, P())
    out_specs = (P(ALL), P(ALL), spec)
    return jax.shard_map(shards, mesh=view, in_specs=in_specs, out_specs=out_specs, check_vma=False)
```

```python
import functools
import math

import jax
import jax.numpy as jnp
from jax import lax
from jax.experimental import pallas as pl
from jax.experimental.pallas import tpu as pltpu
from jax.sharding import Mesh
from jax.sharding import PartitionSpec as P

inverse_temp = 3.0
epsilon = 1e-06
ALL = ("y", "z", "x", "c")


def logical_shift(word, amount):
    return lax.shift_right_logical(word, jnp.full(word.shape, amount, jnp.int32))


def gumbel_noise(row_ids, cent_ids, salt_word):
    mixed = row_ids * 1103515245 + cent_ids * 739982445 + salt_word
    mixed = mixed ^ logical_shift(mixed, 16)
    mixed = mixed * 2146121005
    mixed = mixed ^ logical_shift(mixed, 15)
    mixed = mixed * 1759714725
    mixed = mixed ^ logical_shift(mixed, 16)
    low_bits = mixed & 8388607
    uniform = (low_bits.astype(jnp.float32) + 0.5) * (1.0 / 8388608.0)
    return -jnp.log(-jnp.log(uniform))


def gather_kernel(axes, sizes, x_ref, out_ref, send_sem, recv_sem, local_sem):
    n = math.prod(sizes)
    where = {a: lax.axis_index(a) for a in ALL}
    me = 0
    for a, size in zip(axes, sizes):
        me = me * size + where[a]

    def device_of(index):
        coords = dict(where)
        for a, size in reversed(list(zip(axes, sizes))):
            coords[a] = lax.rem(index, size)
            index = index // size
        return tuple(coords[a] for a in ALL)

    peers = [lax.rem(me + k, n) for k in range(n)]
    barrier = pltpu.get_barrier_semaphore()
    for k in range(1, n):
        pl.semaphore_signal(barrier, inc=1, device_id=device_of(peers[k]), device_id_type=pl.DeviceIdType.MESH)
    pl.semaphore_wait(barrier, n - 1)
    local = pltpu.make_async_copy(x_ref, out_ref.at[me], local_sem)
    local.start()
    sends = []
    for k in range(1, n):
        copy = pltpu.make_async_remote_copy(
            src_ref=x_ref,
            dst_ref=out_ref.at[me],
            send_sem=send_sem.at[k],
            recv_sem=recv_sem.at[me],
            device_id=device_of(peers[k]),
            device_id_type=pl.DeviceIdType.MESH,
        )
        copy.start()
        sends.append(copy)
    for k in range(1, n):
        source = lax.rem(me + n - k, n)
        pltpu.make_async_remote_copy(
            src_ref=x_ref,
            dst_ref=out_ref.at[source],
            send_sem=send_sem.at[k],
            recv_sem=recv_sem.at[source],
            device_id=device_of(source),
            device_id_type=pl.DeviceIdType.MESH,
        ).wait_recv()
    for copy in sends:
        copy.wait_send()
    local.wait()


def gather(x, axes, collective_id):
    sizes = tuple(lax.axis_size(a) for a in axes)
    n = math.prod(sizes)
    out = pl.pallas_call(
        functools.partial(gather_kernel, axes, sizes),
        out_shape=jax.ShapeDtypeStruct((n,) + x.shape, x.dtype),
        in_specs=[pl.BlockSpec(memory_space=pl.ANY)],
        out_specs=pl.BlockSpec(memory_space=pl.ANY),
        scratch_shapes=[
            pltpu.SemaphoreType.DMA((n,)),
            pltpu.SemaphoreType.DMA((n,)),
            pltpu.SemaphoreType.DMA,
        ],
        compiler_params=pltpu.CompilerParams(collective_id=collective_id, has_side_effects=True),
    )(x)
    return out.reshape((n * x.shape[0],) + x.shape[1:])


def cluster_stats(members, valid):
    feature_dim = members.shape[1]
    widened = members.astype(jnp.float32)
    scale = lax.rsqrt(jnp.mean(widened * widened, axis=1) + epsilon)
    gram = lax.dot_general(
        members, members, (((1,), (1,)), ((), ())), preferred_element_type=jnp.float32
    )
    similar = gram * scale[:, None] * scale[None, :] * (1.0 / math.sqrt(feature_dim))
    order = jnp.arange(members.shape[0], dtype=jnp.int32)
    usable = valid[None, :] & (order[:, None] != order[None, :])
    highest = jnp.max(jnp.where(usable, similar, -1e30), axis=1)
    scores = jnp.where(jnp.any(usable, axis=1), highest, 0.0)
    total = jnp.sum(jnp.where(valid[:, None], widened, 0.0), axis=0)
    center = total * lax.rsqrt(jnp.mean(total * total) + epsilon)
    return (scores, center)


def shards(embeddings, centroids, cluster, noise_salt):
    rows_dev, feature_dim = embeddings.shape
    cent_dev = centroids.shape[0]
    ny, nz, nx, nc = (lax.axis_size(a) for a in ALL)
    devices = ny * nz * nx * nc
    capacity = max(2, 2 * rows_dev // devices)
    iy, iz, ix, ic = (lax.axis_index(a) for a in ALL)
    me = ((iy * nz + iz) * nx + ix) * nc + ic
    salt_word = noise_salt[0]
    swap = [(i, (i + 1) % nc) for i in range(nc)]
    ring_y = [
        embeddings if s == 0 else lax.ppermute(embeddings, "y", [(i, (i + s) % ny) for i in range(ny)])
        for s in range(ny)
    ]
    group = jnp.concatenate(ring_y + [lax.ppermute(p, "c", swap) for p in ring_y], axis=0)
    src_c = jnp.stack([ic, (ic + nc - 1) % nc])
    src_y = (iy - jnp.arange(ny, dtype=jnp.int32)) % ny
    row_dev = ((src_y[None, :] * nz + iz) * nx + ix) * nc + src_c[:, None]
    group_ids = (row_dev[:, :, None] * rows_dev + jnp.arange(rows_dev, dtype=jnp.int32)).reshape(-1)
    halves = 2
    share = cent_dev // halves
    spread = nz * nx
    cpos = jnp.arange(spread * share, dtype=jnp.int32)
    cent_dev_ids = ((iy * nz + cpos // (nx * share)) * nx + cpos // share % nx) * nc + ic
    result = jnp.full((group.shape[0],), -1e30, jnp.float32)

    def step(carry, item):
        tile, noise_tile = item
        scores = lax.dot_general(
            group, tile, (((1,), (1,)), ((), ())), preferred_element_type=jnp.float32
        )
        perturbed = inverse_temp * scores + noise_tile
        return (jnp.maximum(carry, jnp.max(perturbed, axis=1)), None)

    for h in range(halves):
        piece = lax.all_gather(centroids[h * share:(h + 1) * share], ("z", "x"), axis=0, tiled=True)
        cent_ids = cent_dev_ids * cent_dev + h * share + cpos % share
        piece_rows = piece.shape[0]
        block = math.gcd(piece_rows, 512)
        steps = piece_rows // block
        tiles = piece.reshape(steps, block, feature_dim)
        noise = gumbel_noise(group_ids[:, None], cent_ids[None, :], salt_word)
        noise_tiles = noise.reshape(group.shape[0], steps, block).transpose(1, 0, 2)
        result, unused = lax.scan(step, result, (tiles, noise_tiles))
    blocks = result.reshape(nc, ny, rows_dev)
    best = blocks[0, 0]
    for sc in range(nc):
        for sy in range(ny):
            if sc == 0 and sy == 0:
                continue
            perm = [(yy * nc + cc, (yy - sy) % ny * nc + (cc - sc) % nc) for yy in range(ny) for cc in range(nc)]
            best = jnp.maximum(best, lax.ppermute(blocks[sc, sy], ("y", "c"), perm))
    perturbed_max = best
    assigned = cluster[:, 0]
    order = jnp.arange(rows_dev, dtype=jnp.int32)
    same = (assigned[:, None] == assigned[None, :]) & (order[None, :] < order[:, None])
    rank = jnp.sum(same.astype(jnp.int32), axis=1)
    slot = assigned * capacity + rank
    flag_width = 128
    tagged = jnp.concatenate([embeddings, jnp.ones((rows_dev, flag_width), jnp.bfloat16)], axis=1)
    outgoing = jnp.zeros((devices * capacity, feature_dim + flag_width), jnp.bfloat16).at[slot].set(tagged)
    received = lax.all_to_all(
        outgoing.reshape(devices, capacity, feature_dim + flag_width), ALL, split_axis=0, concat_axis=0, tiled=True
    ).reshape(devices * capacity, feature_dim + flag_width)
    members = received[:, :feature_dim]
    valid = received[:, feature_dim] > 0.5
    scores, center = cluster_stats(members, valid)
    returned = lax.all_to_all(
        scores.reshape(devices, capacity), ALL, split_axis=0, concat_axis=0, tiled=True
    )
    dedup_score = returned.reshape(devices * capacity)[slot]
    return (perturbed_max, dedup_score, center[None, :])


def solution(mesh):
    cent_count, rows_count = mesh.devices.shape
    cores = 2
    side = math.isqrt(rows_count // cores)
    view = Mesh(mesh.devices.reshape(cent_count, side, rows_count // cores // side, cores), ALL)
    spec = P(ALL, None)
    in_specs = (spec, spec, spec, P())
    out_specs = (P(ALL), P(ALL), spec)
    return jax.shard_map(shards, mesh=view, in_specs=in_specs, out_specs=out_specs, check_vma=False)
```

```python
import functools
import math

import jax
import jax.numpy as jnp
from jax import lax
from jax.experimental import pallas as pl
from jax.experimental.pallas import tpu as pltpu
from jax.sharding import Mesh
from jax.sharding import PartitionSpec as P

inverse_temp = 3.0
epsilon = 1e-06
ALL = ("y", "z", "x", "c")


def logical_shift(word, amount):
    return lax.shift_right_logical(word, jnp.full(word.shape, amount, jnp.int32))


def gumbel_noise(row_ids, cent_ids, salt_word):
    mixed = row_ids * 1103515245 + cent_ids * 739982445 + salt_word
    mixed = mixed ^ logical_shift(mixed, 16)
    mixed = mixed * 2146121005
    mixed = mixed ^ logical_shift(mixed, 15)
    mixed = mixed * 1759714725
    mixed = mixed ^ logical_shift(mixed, 16)
    low_bits = mixed & 8388607
    uniform = (low_bits.astype(jnp.float32) + 0.5) * (1.0 / 8388608.0)
    return -jnp.log(-jnp.log(uniform))


def gather_kernel(axes, sizes, x_ref, out_ref, send_sem, recv_sem, local_sem):
    n = math.prod(sizes)
    where = {a: lax.axis_index(a) for a in ALL}
    me = 0
    for a, size in zip(axes, sizes):
        me = me * size + where[a]

    def device_of(index):
        coords = dict(where)
        for a, size in reversed(list(zip(axes, sizes))):
            coords[a] = lax.rem(index, size)
            index = index // size
        return tuple(coords[a] for a in ALL)

    peers = [lax.rem(me + k, n) for k in range(n)]
    barrier = pltpu.get_barrier_semaphore()
    for k in range(1, n):
        pl.semaphore_signal(barrier, inc=1, device_id=device_of(peers[k]), device_id_type=pl.DeviceIdType.MESH)
    pl.semaphore_wait(barrier, n - 1)
    local = pltpu.make_async_copy(x_ref, out_ref.at[me], local_sem)
    local.start()
    sends = []
    for k in range(1, n):
        copy = pltpu.make_async_remote_copy(
            src_ref=x_ref,
            dst_ref=out_ref.at[me],
            send_sem=send_sem.at[k],
            recv_sem=recv_sem.at[me],
            device_id=device_of(peers[k]),
            device_id_type=pl.DeviceIdType.MESH,
        )
        copy.start()
        sends.append(copy)
    for k in range(1, n):
        source = lax.rem(me + n - k, n)
        pltpu.make_async_remote_copy(
            src_ref=x_ref,
            dst_ref=out_ref.at[source],
            send_sem=send_sem.at[k],
            recv_sem=recv_sem.at[source],
            device_id=device_of(source),
            device_id_type=pl.DeviceIdType.MESH,
        ).wait_recv()
    for copy in sends:
        copy.wait_send()
    local.wait()


def gather(x, axes, collective_id):
    sizes = tuple(lax.axis_size(a) for a in axes)
    n = math.prod(sizes)
    out = pl.pallas_call(
        functools.partial(gather_kernel, axes, sizes),
        out_shape=jax.ShapeDtypeStruct((n,) + x.shape, x.dtype),
        in_specs=[pl.BlockSpec(memory_space=pl.ANY)],
        out_specs=pl.BlockSpec(memory_space=pl.ANY),
        scratch_shapes=[
            pltpu.SemaphoreType.DMA((n,)),
            pltpu.SemaphoreType.DMA((n,)),
            pltpu.SemaphoreType.DMA,
        ],
        compiler_params=pltpu.CompilerParams(collective_id=collective_id, has_side_effects=True),
    )(x)
    return out.reshape((n * x.shape[0],) + x.shape[1:])


def cluster_stats(members, valid):
    feature_dim = members.shape[1]
    widened = members.astype(jnp.float32)
    scale = lax.rsqrt(jnp.mean(widened * widened, axis=1) + epsilon)
    gram = lax.dot_general(
        members, members, (((1,), (1,)), ((), ())), preferred_element_type=jnp.float32
    )
    similar = gram * scale[:, None] * scale[None, :] * (1.0 / math.sqrt(feature_dim))
    order = jnp.arange(members.shape[0], dtype=jnp.int32)
    usable = valid[None, :] & (order[:, None] != order[None, :])
    highest = jnp.max(jnp.where(usable, similar, -1e30), axis=1)
    scores = jnp.where(jnp.any(usable, axis=1), highest, 0.0)
    total = jnp.sum(jnp.where(valid[:, None], widened, 0.0), axis=0)
    center = total * lax.rsqrt(jnp.mean(total * total) + epsilon)
    return (scores, center)


def shards(embeddings, centroids, cluster, noise_salt):
    rows_dev, feature_dim = embeddings.shape
    cent_dev = centroids.shape[0]
    ny, nz, nx, nc = (lax.axis_size(a) for a in ALL)
    devices = ny * nz * nx * nc
    capacity = max(2, 2 * rows_dev // devices)
    iy, iz, ix, ic = (lax.axis_index(a) for a in ALL)
    me = ((iy * nz + iz) * nx + ix) * nc + ic
    salt_word = noise_salt[0]
    swap = [(i, (i + 1) % nc) for i in range(nc)]
    def shift_y(x, s):
        return lax.ppermute(x, "y", [(i, (i + s) % ny) for i in range(ny)])

    ring_y = []
    for s in range(ny):
        if s == 0:
            ring_y.append(embeddings)
        elif 2 * s == ny:
            cut = rows_dev // 2
            ahead, behind = embeddings[:cut], embeddings[cut:]
            for unused in range(s):
                ahead, behind = shift_y(ahead, 1), shift_y(behind, -1)
            ring_y.append(jnp.concatenate([ahead, behind], axis=0))
        else:
            ring_y.append(shift_y(embeddings, s))
    group = jnp.concatenate(ring_y + [lax.ppermute(p, "c", swap) for p in ring_y], axis=0)
    src_c = jnp.stack([ic, (ic + nc - 1) % nc])
    src_y = (iy - jnp.arange(ny, dtype=jnp.int32)) % ny
    row_dev = ((src_y[None, :] * nz + iz) * nx + ix) * nc + src_c[:, None]
    group_ids = (row_dev[:, :, None] * rows_dev + jnp.arange(rows_dev, dtype=jnp.int32)).reshape(-1)
    halves = 2
    share = cent_dev // halves
    spread = nz * nx
    cpos = jnp.arange(spread * share, dtype=jnp.int32)
    cent_dev_ids = ((iy * nz + cpos // (nx * share)) * nx + cpos // share % nx) * nc + ic
    result = jnp.full((group.shape[0],), -1e30, jnp.float32)

    def step(carry, item):
        tile, noise_tile = item
        scores = lax.dot_general(
            group, tile, (((1,), (1,)), ((), ())), preferred_element_type=jnp.float32
        )
        perturbed = inverse_temp * scores + noise_tile
        return (jnp.maximum(carry, jnp.max(perturbed, axis=1)), None)

    for h in range(halves):
        piece = lax.all_gather(centroids[h * share:(h + 1) * share], ("z", "x"), axis=0, tiled=True)
        cent_ids = cent_dev_ids * cent_dev + h * share + cpos % share
        piece_rows = piece.shape[0]
        block = math.gcd(piece_rows, 512)
        steps = piece_rows // block
        tiles = piece.reshape(steps, block, feature_dim)
        noise = gumbel_noise(group_ids[:, None], cent_ids[None, :], salt_word)
        noise_tiles = noise.reshape(group.shape[0], steps, block).transpose(1, 0, 2)
        result, unused = lax.scan(step, result, (tiles, noise_tiles))
    blocks = result.reshape(nc, ny, rows_dev)
    best = blocks[0, 0]
    for sc in range(nc):
        for sy in range(ny):
            if sc == 0 and sy == 0:
                continue
            perm = [(yy * nc + cc, (yy - sy) % ny * nc + (cc - sc) % nc) for yy in range(ny) for cc in range(nc)]
            best = jnp.maximum(best, lax.ppermute(blocks[sc, sy], ("y", "c"), perm))
    perturbed_max = best
    assigned = cluster[:, 0]
    order = jnp.arange(rows_dev, dtype=jnp.int32)
    same = (assigned[:, None] == assigned[None, :]) & (order[None, :] < order[:, None])
    rank = jnp.sum(same.astype(jnp.int32), axis=1)
    slot = assigned * capacity + rank
    flag_width = 128
    tagged = jnp.concatenate([embeddings, jnp.ones((rows_dev, flag_width), jnp.bfloat16)], axis=1)
    outgoing = jnp.zeros((devices * capacity, feature_dim + flag_width), jnp.bfloat16).at[slot].set(tagged)
    received = lax.all_to_all(
        outgoing.reshape(devices, capacity, feature_dim + flag_width), ALL, split_axis=0, concat_axis=0, tiled=True
    ).reshape(devices * capacity, feature_dim + flag_width)
    members = received[:, :feature_dim]
    valid = received[:, feature_dim] > 0.5
    scores, center = cluster_stats(members, valid)
    returned = lax.all_to_all(
        scores.reshape(devices, capacity), ALL, split_axis=0, concat_axis=0, tiled=True
    )
    dedup_score = returned.reshape(devices * capacity)[slot]
    return (perturbed_max, dedup_score, center[None, :])


def solution(mesh):
    cent_count, rows_count = mesh.devices.shape
    cores = 2
    side = math.isqrt(rows_count // cores)
    view = Mesh(mesh.devices.reshape(cent_count, side, rows_count // cores // side, cores), ALL)
    spec = P(ALL, None)
    in_specs = (spec, spec, spec, P())
    out_specs = (P(ALL), P(ALL), spec)
    return jax.shard_map(shards, mesh=view, in_specs=in_specs, out_specs=out_specs, check_vma=False)
```

```python
import functools
import math

import jax
import jax.numpy as jnp
from jax import lax
from jax.experimental import pallas as pl
from jax.experimental.pallas import tpu as pltpu
from jax.sharding import Mesh
from jax.sharding import PartitionSpec as P

inverse_temp = 3.0
epsilon = 1e-06
ALL = ("y", "z", "x", "c")


def logical_shift(word, amount):
    return lax.shift_right_logical(word, jnp.full(word.shape, amount, jnp.int32))


def gumbel_noise(row_ids, cent_ids, salt_word):
    mixed = row_ids * 1103515245 + cent_ids * 739982445 + salt_word
    mixed = mixed ^ logical_shift(mixed, 16)
    mixed = mixed * 2146121005
    mixed = mixed ^ logical_shift(mixed, 15)
    mixed = mixed * 1759714725
    mixed = mixed ^ logical_shift(mixed, 16)
    low_bits = mixed & 8388607
    uniform = (low_bits.astype(jnp.float32) + 0.5) * (1.0 / 8388608.0)
    return -jnp.log(-jnp.log(uniform))


def gather_kernel(axes, sizes, x_ref, out_ref, send_sem, recv_sem, local_sem):
    n = math.prod(sizes)
    where = {a: lax.axis_index(a) for a in ALL}
    me = 0
    for a, size in zip(axes, sizes):
        me = me * size + where[a]

    def device_of(index):
        coords = dict(where)
        for a, size in reversed(list(zip(axes, sizes))):
            coords[a] = lax.rem(index, size)
            index = index // size
        return tuple(coords[a] for a in ALL)

    peers = [lax.rem(me + k, n) for k in range(n)]
    barrier = pltpu.get_barrier_semaphore()
    for k in range(1, n):
        pl.semaphore_signal(barrier, inc=1, device_id=device_of(peers[k]), device_id_type=pl.DeviceIdType.MESH)
    pl.semaphore_wait(barrier, n - 1)
    local = pltpu.make_async_copy(x_ref, out_ref.at[me], local_sem)
    local.start()
    sends = []
    for k in range(1, n):
        copy = pltpu.make_async_remote_copy(
            src_ref=x_ref,
            dst_ref=out_ref.at[me],
            send_sem=send_sem.at[k],
            recv_sem=recv_sem.at[me],
            device_id=device_of(peers[k]),
            device_id_type=pl.DeviceIdType.MESH,
        )
        copy.start()
        sends.append(copy)
    for k in range(1, n):
        source = lax.rem(me + n - k, n)
        pltpu.make_async_remote_copy(
            src_ref=x_ref,
            dst_ref=out_ref.at[source],
            send_sem=send_sem.at[k],
            recv_sem=recv_sem.at[source],
            device_id=device_of(source),
            device_id_type=pl.DeviceIdType.MESH,
        ).wait_recv()
    for copy in sends:
        copy.wait_send()
    local.wait()


def gather(x, axes, collective_id):
    sizes = tuple(lax.axis_size(a) for a in axes)
    n = math.prod(sizes)
    out = pl.pallas_call(
        functools.partial(gather_kernel, axes, sizes),
        out_shape=jax.ShapeDtypeStruct((n,) + x.shape, x.dtype),
        in_specs=[pl.BlockSpec(memory_space=pl.ANY)],
        out_specs=pl.BlockSpec(memory_space=pl.ANY),
        scratch_shapes=[
            pltpu.SemaphoreType.DMA((n,)),
            pltpu.SemaphoreType.DMA((n,)),
            pltpu.SemaphoreType.DMA,
        ],
        compiler_params=pltpu.CompilerParams(collective_id=collective_id, has_side_effects=True),
    )(x)
    return out.reshape((n * x.shape[0],) + x.shape[1:])


def score_kernel(rows_ref, cents_ref, noise_ref, out_ref):
    scores = lax.dot_general(
        rows_ref[...], cents_ref[...], (((1,), (1,)), ((), ())), preferred_element_type=jnp.float32
    )
    best = jnp.max(inverse_temp * scores + noise_ref[...], axis=1, keepdims=True)

    @pl.when(pl.program_id(1) == 0)
    def _():
        out_ref[...] = best

    @pl.when(pl.program_id(1) > 0)
    def _():
        out_ref[...] = jnp.maximum(out_ref[...], best)


def score_max(rows, cents, noise):
    count, width = rows.shape
    tm = min(512, count)
    tn = min(512, cents.shape[0])
    out = pl.pallas_call(
        score_kernel,
        out_shape=jax.ShapeDtypeStruct((count, 1), jnp.float32),
        grid=(count // tm, cents.shape[0] // tn),
        in_specs=[
            pl.BlockSpec((tm, width), lambda i, j: (i, 0)),
            pl.BlockSpec((tn, width), lambda i, j: (j, 0)),
            pl.BlockSpec((tm, tn), lambda i, j: (i, j)),
        ],
        out_specs=pl.BlockSpec((tm, 1), lambda i, j: (i, 0)),
        compiler_params=pltpu.CompilerParams(dimension_semantics=("parallel", "arbitrary")),
    )(rows, cents, noise)
    return out[:, 0]


def cluster_stats(members, valid):
    feature_dim = members.shape[1]
    widened = members.astype(jnp.float32)
    scale = lax.rsqrt(jnp.mean(widened * widened, axis=1) + epsilon)
    gram = lax.dot_general(
        members, members, (((1,), (1,)), ((), ())), preferred_element_type=jnp.float32
    )
    similar = gram * scale[:, None] * scale[None, :] * (1.0 / math.sqrt(feature_dim))
    order = jnp.arange(members.shape[0], dtype=jnp.int32)
    usable = valid[None, :] & (order[:, None] != order[None, :])
    highest = jnp.max(jnp.where(usable, similar, -1e30), axis=1)
    scores = jnp.where(jnp.any(usable, axis=1), highest, 0.0)
    total = jnp.sum(jnp.where(valid[:, None], widened, 0.0), axis=0)
    center = total * lax.rsqrt(jnp.mean(total * total) + epsilon)
    return (scores, center)


def shards(embeddings, centroids, cluster, noise_salt):
    rows_dev, feature_dim = embeddings.shape
    cent_dev = centroids.shape[0]
    ny, nz, nx, nc = (lax.axis_size(a) for a in ALL)
    devices = ny * nz * nx * nc
    capacity = max(2, 2 * rows_dev // devices)
    iy, iz, ix, ic = (lax.axis_index(a) for a in ALL)
    me = ((iy * nz + iz) * nx + ix) * nc + ic
    salt_word = noise_salt[0]
    swap = [(i, (i + 1) % nc) for i in range(nc)]
    ring_y = [
        embeddings if s == 0 else lax.ppermute(embeddings, "y", [(i, (i + s) % ny) for i in range(ny)])
        for s in range(ny)
    ]
    group = jnp.concatenate(ring_y + [lax.ppermute(p, "c", swap) for p in ring_y], axis=0)
    piece = lax.all_gather(centroids, ("z", "x"), axis=0, tiled=True)
    src_c = jnp.stack([ic, (ic + nc - 1) % nc])
    src_y = (iy - jnp.arange(ny, dtype=jnp.int32)) % ny
    row_dev = ((src_y[None, :] * nz + iz) * nx + ix) * nc + src_c[:, None]
    group_ids = (row_dev[:, :, None] * rows_dev + jnp.arange(rows_dev, dtype=jnp.int32)).reshape(-1)
    cpos = jnp.arange(nz * nx * cent_dev, dtype=jnp.int32)
    cent_dev_ids = ((iy * nz + cpos // (nx * cent_dev)) * nx + cpos // cent_dev % nx) * nc + ic
    cent_ids = cent_dev_ids * cent_dev + cpos % cent_dev
    noise = gumbel_noise(group_ids[:, None], cent_ids[None, :], salt_word)
    result = score_max(group, piece, noise)
    blocks = result.reshape(nc, ny, rows_dev)
    best = blocks[0, 0]
    for sc in range(nc):
        for sy in range(ny):
            if sc == 0 and sy == 0:
                continue
            perm = [(yy * nc + cc, (yy - sy) % ny * nc + (cc - sc) % nc) for yy in range(ny) for cc in range(nc)]
            best = jnp.maximum(best, lax.ppermute(blocks[sc, sy], ("y", "c"), perm))
    perturbed_max = best
    assigned = cluster[:, 0]
    order = jnp.arange(rows_dev, dtype=jnp.int32)
    same = (assigned[:, None] == assigned[None, :]) & (order[None, :] < order[:, None])
    rank = jnp.sum(same.astype(jnp.int32), axis=1)
    slot = assigned * capacity + rank
    flag_width = 128
    tagged = jnp.concatenate([embeddings, jnp.ones((rows_dev, flag_width), jnp.bfloat16)], axis=1)
    outgoing = jnp.zeros((devices * capacity, feature_dim + flag_width), jnp.bfloat16).at[slot].set(tagged)
    received = lax.all_to_all(
        outgoing.reshape(devices, capacity, feature_dim + flag_width), ALL, split_axis=0, concat_axis=0, tiled=True
    ).reshape(devices * capacity, feature_dim + flag_width)
    members = received[:, :feature_dim]
    valid = received[:, feature_dim] > 0.5
    scores, center = cluster_stats(members, valid)
    returned = lax.all_to_all(
        scores.reshape(devices, capacity), ALL, split_axis=0, concat_axis=0, tiled=True
    )
    dedup_score = returned.reshape(devices * capacity)[slot]
    return (perturbed_max, dedup_score, center[None, :])


def solution(mesh):
    cent_count, rows_count = mesh.devices.shape
    cores = 2
    side = math.isqrt(rows_count // cores)
    view = Mesh(mesh.devices.reshape(cent_count, side, rows_count // cores // side, cores), ALL)
    spec = P(ALL, None)
    in_specs = (spec, spec, spec, P())
    out_specs = (P(ALL), P(ALL), spec)
    return jax.shard_map(shards, mesh=view, in_specs=in_specs, out_specs=out_specs, check_vma=False)
```

```python
import functools
import math

import jax
import jax.numpy as jnp
from jax import lax
from jax.experimental import pallas as pl
from jax.experimental.pallas import tpu as pltpu
from jax.sharding import Mesh
from jax.sharding import PartitionSpec as P

inverse_temp = 3.0
epsilon = 1e-06
ALL = ("y", "z", "x", "c")


def logical_shift(word, amount):
    return lax.shift_right_logical(word, jnp.full(word.shape, amount, jnp.int32))


def gumbel_noise(row_ids, cent_ids, salt_word):
    mixed = row_ids * 1103515245 + cent_ids * 739982445 + salt_word
    mixed = mixed ^ logical_shift(mixed, 16)
    mixed = mixed * 2146121005
    mixed = mixed ^ logical_shift(mixed, 15)
    mixed = mixed * 1759714725
    mixed = mixed ^ logical_shift(mixed, 16)
    low_bits = mixed & 8388607
    uniform = (low_bits.astype(jnp.float32) + 0.5) * (1.0 / 8388608.0)
    return -jnp.log(-jnp.log(uniform))


def gather_kernel(axes, sizes, x_ref, out_ref, send_sem, recv_sem, local_sem):
    n = math.prod(sizes)
    where = {a: lax.axis_index(a) for a in ALL}
    me = 0
    for a, size in zip(axes, sizes):
        me = me * size + where[a]

    def device_of(index):
        coords = dict(where)
        for a, size in reversed(list(zip(axes, sizes))):
            coords[a] = lax.rem(index, size)
            index = index // size
        return tuple(coords[a] for a in ALL)

    peers = [lax.rem(me + k, n) for k in range(n)]
    barrier = pltpu.get_barrier_semaphore()
    for k in range(1, n):
        pl.semaphore_signal(barrier, inc=1, device_id=device_of(peers[k]), device_id_type=pl.DeviceIdType.MESH)
    pl.semaphore_wait(barrier, n - 1)
    local = pltpu.make_async_copy(x_ref, out_ref.at[me], local_sem)
    local.start()
    sends = []
    for k in range(1, n):
        copy = pltpu.make_async_remote_copy(
            src_ref=x_ref,
            dst_ref=out_ref.at[me],
            send_sem=send_sem.at[k],
            recv_sem=recv_sem.at[me],
            device_id=device_of(peers[k]),
            device_id_type=pl.DeviceIdType.MESH,
        )
        copy.start()
        sends.append(copy)
    for k in range(1, n):
        source = lax.rem(me + n - k, n)
        pltpu.make_async_remote_copy(
            src_ref=x_ref,
            dst_ref=out_ref.at[source],
            send_sem=send_sem.at[k],
            recv_sem=recv_sem.at[source],
            device_id=device_of(source),
            device_id_type=pl.DeviceIdType.MESH,
        ).wait_recv()
    for copy in sends:
        copy.wait_send()
    local.wait()


def gather(x, axes, collective_id):
    sizes = tuple(lax.axis_size(a) for a in axes)
    n = math.prod(sizes)
    out = pl.pallas_call(
        functools.partial(gather_kernel, axes, sizes),
        out_shape=jax.ShapeDtypeStruct((n,) + x.shape, x.dtype),
        in_specs=[pl.BlockSpec(memory_space=pl.ANY)],
        out_specs=pl.BlockSpec(memory_space=pl.ANY),
        scratch_shapes=[
            pltpu.SemaphoreType.DMA((n,)),
            pltpu.SemaphoreType.DMA((n,)),
            pltpu.SemaphoreType.DMA,
        ],
        compiler_params=pltpu.CompilerParams(collective_id=collective_id, has_side_effects=True),
    )(x)
    return out.reshape((n * x.shape[0],) + x.shape[1:])


def score_kernel(rows_ref, cents_ref, noise_ref, out_ref):
    scores = lax.dot_general(
        rows_ref[...], cents_ref[...], (((1,), (1,)), ((), ())), preferred_element_type=jnp.float32
    )
    best = jnp.max(inverse_temp * scores + noise_ref[...], axis=1, keepdims=True)

    @pl.when(pl.program_id(1) == 0)
    def _():
        out_ref[...] = best

    @pl.when(pl.program_id(1) > 0)
    def _():
        out_ref[...] = jnp.maximum(out_ref[...], best)


def score_max(rows, cents, noise):
    count, width = rows.shape
    tm = min(1024, count)
    tn = min(512, cents.shape[0])
    out = pl.pallas_call(
        score_kernel,
        out_shape=jax.ShapeDtypeStruct((count, 1), jnp.float32),
        grid=(count // tm, cents.shape[0] // tn),
        in_specs=[
            pl.BlockSpec((tm, width), lambda i, j: (i, 0)),
            pl.BlockSpec((tn, width), lambda i, j: (j, 0)),
            pl.BlockSpec((tm, tn), lambda i, j: (i, j)),
        ],
        out_specs=pl.BlockSpec((tm, 1), lambda i, j: (i, 0)),
        compiler_params=pltpu.CompilerParams(dimension_semantics=("parallel", "arbitrary")),
    )(rows, cents, noise)
    return out[:, 0]


def cluster_stats(members, valid):
    feature_dim = members.shape[1]
    widened = members.astype(jnp.float32)
    scale = lax.rsqrt(jnp.mean(widened * widened, axis=1) + epsilon)
    gram = lax.dot_general(
        members, members, (((1,), (1,)), ((), ())), preferred_element_type=jnp.float32
    )
    similar = gram * scale[:, None] * scale[None, :] * (1.0 / math.sqrt(feature_dim))
    order = jnp.arange(members.shape[0], dtype=jnp.int32)
    usable = valid[None, :] & (order[:, None] != order[None, :])
    highest = jnp.max(jnp.where(usable, similar, -1e30), axis=1)
    scores = jnp.where(jnp.any(usable, axis=1), highest, 0.0)
    total = jnp.sum(jnp.where(valid[:, None], widened, 0.0), axis=0)
    center = total * lax.rsqrt(jnp.mean(total * total) + epsilon)
    return (scores, center)


def shards(embeddings, centroids, cluster, noise_salt):
    rows_dev, feature_dim = embeddings.shape
    cent_dev = centroids.shape[0]
    ny, nz, nx, nc = (lax.axis_size(a) for a in ALL)
    devices = ny * nz * nx * nc
    capacity = max(2, 2 * rows_dev // devices)
    iy, iz, ix, ic = (lax.axis_index(a) for a in ALL)
    me = ((iy * nz + iz) * nx + ix) * nc + ic
    salt_word = noise_salt[0]
    swap = [(i, (i + 1) % nc) for i in range(nc)]
    ring_y = [
        embeddings if s == 0 else lax.ppermute(embeddings, "y", [(i, (i + s) % ny) for i in range(ny)])
        for s in range(ny)
    ]
    group = jnp.concatenate(ring_y + [lax.ppermute(p, "c", swap) for p in ring_y], axis=0)
    piece = lax.all_gather(centroids, ("z", "x"), axis=0, tiled=True)
    src_c = jnp.stack([ic, (ic + nc - 1) % nc])
    src_y = (iy - jnp.arange(ny, dtype=jnp.int32)) % ny
    row_dev = ((src_y[None, :] * nz + iz) * nx + ix) * nc + src_c[:, None]
    group_ids = (row_dev[:, :, None] * rows_dev + jnp.arange(rows_dev, dtype=jnp.int32)).reshape(-1)
    cpos = jnp.arange(nz * nx * cent_dev, dtype=jnp.int32)
    cent_dev_ids = ((iy * nz + cpos // (nx * cent_dev)) * nx + cpos // cent_dev % nx) * nc + ic
    cent_ids = cent_dev_ids * cent_dev + cpos % cent_dev
    noise = gumbel_noise(group_ids[:, None], cent_ids[None, :], salt_word)
    result = score_max(group, piece, noise)
    blocks = result.reshape(nc, ny, rows_dev)
    best = blocks[0, 0]
    for sc in range(nc):
        for sy in range(ny):
            if sc == 0 and sy == 0:
                continue
            perm = [(yy * nc + cc, (yy - sy) % ny * nc + (cc - sc) % nc) for yy in range(ny) for cc in range(nc)]
            best = jnp.maximum(best, lax.ppermute(blocks[sc, sy], ("y", "c"), perm))
    perturbed_max = best
    assigned = cluster[:, 0]
    order = jnp.arange(rows_dev, dtype=jnp.int32)
    same = (assigned[:, None] == assigned[None, :]) & (order[None, :] < order[:, None])
    rank = jnp.sum(same.astype(jnp.int32), axis=1)
    slot = assigned * capacity + rank
    flag_width = 128
    tagged = jnp.concatenate([embeddings, jnp.ones((rows_dev, flag_width), jnp.bfloat16)], axis=1)
    outgoing = jnp.zeros((devices * capacity, feature_dim + flag_width), jnp.bfloat16).at[slot].set(tagged)
    received = lax.all_to_all(
        outgoing.reshape(devices, capacity, feature_dim + flag_width), ALL, split_axis=0, concat_axis=0, tiled=True
    ).reshape(devices * capacity, feature_dim + flag_width)
    members = received[:, :feature_dim]
    valid = received[:, feature_dim] > 0.5
    scores, center = cluster_stats(members, valid)
    returned = lax.all_to_all(
        scores.reshape(devices, capacity), ALL, split_axis=0, concat_axis=0, tiled=True
    )
    dedup_score = returned.reshape(devices * capacity)[slot]
    return (perturbed_max, dedup_score, center[None, :])


def solution(mesh):
    cent_count, rows_count = mesh.devices.shape
    cores = 2
    side = math.isqrt(rows_count // cores)
    view = Mesh(mesh.devices.reshape(cent_count, side, rows_count // cores // side, cores), ALL)
    spec = P(ALL, None)
    in_specs = (spec, spec, spec, P())
    out_specs = (P(ALL), P(ALL), spec)
    return jax.shard_map(shards, mesh=view, in_specs=in_specs, out_specs=out_specs, check_vma=False)
```

```python
import functools
import math

import jax
import jax.numpy as jnp
from jax import lax
from jax.experimental import pallas as pl
from jax.experimental.pallas import tpu as pltpu
from jax.sharding import Mesh
from jax.sharding import PartitionSpec as P

inverse_temp = 3.0
epsilon = 1e-06
ALL = ("y", "z", "x", "c")


def logical_shift(word, amount):
    return lax.shift_right_logical(word, jnp.full(word.shape, amount, jnp.int32))


def gumbel_noise(row_ids, cent_ids, salt_word):
    mixed = row_ids * 1103515245 + cent_ids * 739982445 + salt_word
    mixed = mixed ^ logical_shift(mixed, 16)
    mixed = mixed * 2146121005
    mixed = mixed ^ logical_shift(mixed, 15)
    mixed = mixed * 1759714725
    mixed = mixed ^ logical_shift(mixed, 16)
    low_bits = mixed & 8388607
    uniform = (low_bits.astype(jnp.float32) + 0.5) * (1.0 / 8388608.0)
    return -jnp.log(-jnp.log(uniform))


def gather_kernel(axes, sizes, x_ref, out_ref, send_sem, recv_sem, local_sem):
    n = math.prod(sizes)
    where = {a: lax.axis_index(a) for a in ALL}
    me = 0
    for a, size in zip(axes, sizes):
        me = me * size + where[a]

    def device_of(index):
        coords = dict(where)
        for a, size in reversed(list(zip(axes, sizes))):
            coords[a] = lax.rem(index, size)
            index = index // size
        return tuple(coords[a] for a in ALL)

    peers = [lax.rem(me + k, n) for k in range(n)]
    barrier = pltpu.get_barrier_semaphore()
    for k in range(1, n):
        pl.semaphore_signal(barrier, inc=1, device_id=device_of(peers[k]), device_id_type=pl.DeviceIdType.MESH)
    pl.semaphore_wait(barrier, n - 1)
    local = pltpu.make_async_copy(x_ref, out_ref.at[me], local_sem)
    local.start()
    sends = []
    for k in range(1, n):
        copy = pltpu.make_async_remote_copy(
            src_ref=x_ref,
            dst_ref=out_ref.at[me],
            send_sem=send_sem.at[k],
            recv_sem=recv_sem.at[me],
            device_id=device_of(peers[k]),
            device_id_type=pl.DeviceIdType.MESH,
        )
        copy.start()
        sends.append(copy)
    for k in range(1, n):
        source = lax.rem(me + n - k, n)
        pltpu.make_async_remote_copy(
            src_ref=x_ref,
            dst_ref=out_ref.at[source],
            send_sem=send_sem.at[k],
            recv_sem=recv_sem.at[source],
            device_id=device_of(source),
            device_id_type=pl.DeviceIdType.MESH,
        ).wait_recv()
    for copy in sends:
        copy.wait_send()
    local.wait()


def gather(x, axes, collective_id):
    sizes = tuple(lax.axis_size(a) for a in axes)
    n = math.prod(sizes)
    out = pl.pallas_call(
        functools.partial(gather_kernel, axes, sizes),
        out_shape=jax.ShapeDtypeStruct((n,) + x.shape, x.dtype),
        in_specs=[pl.BlockSpec(memory_space=pl.ANY)],
        out_specs=pl.BlockSpec(memory_space=pl.ANY),
        scratch_shapes=[
            pltpu.SemaphoreType.DMA((n,)),
            pltpu.SemaphoreType.DMA((n,)),
            pltpu.SemaphoreType.DMA,
        ],
        compiler_params=pltpu.CompilerParams(collective_id=collective_id, has_side_effects=True),
    )(x)
    return out.reshape((n * x.shape[0],) + x.shape[1:])


def score_kernel(rows_ref, cents_ref, noise_ref, out_ref):
    scores = lax.dot_general(
        rows_ref[...], cents_ref[...], (((1,), (1,)), ((), ())), preferred_element_type=jnp.float32
    )
    best = jnp.max(inverse_temp * scores + noise_ref[...], axis=1, keepdims=True)

    @pl.when(pl.program_id(1) == 0)
    def _():
        out_ref[...] = best

    @pl.when(pl.program_id(1) > 0)
    def _():
        out_ref[...] = jnp.maximum(out_ref[...], best)


def score_max(rows, cents, noise):
    count, width = rows.shape
    tm = min(2048, count)
    tn = min(256, cents.shape[0])
    out = pl.pallas_call(
        score_kernel,
        out_shape=jax.ShapeDtypeStruct((count, 1), jnp.float32),
        grid=(count // tm, cents.shape[0] // tn),
        in_specs=[
            pl.BlockSpec((tm, width), lambda i, j: (i, 0)),
            pl.BlockSpec((tn, width), lambda i, j: (j, 0)),
            pl.BlockSpec((tm, tn), lambda i, j: (i, j)),
        ],
        out_specs=pl.BlockSpec((tm, 1), lambda i, j: (i, 0)),
        compiler_params=pltpu.CompilerParams(dimension_semantics=("parallel", "arbitrary")),
    )(rows, cents, noise)
    return out[:, 0]


def cluster_stats(members, valid):
    feature_dim = members.shape[1]
    widened = members.astype(jnp.float32)
    scale = lax.rsqrt(jnp.mean(widened * widened, axis=1) + epsilon)
    gram = lax.dot_general(
        members, members, (((1,), (1,)), ((), ())), preferred_element_type=jnp.float32
    )
    similar = gram * scale[:, None] * scale[None, :] * (1.0 / math.sqrt(feature_dim))
    order = jnp.arange(members.shape[0], dtype=jnp.int32)
    usable = valid[None, :] & (order[:, None] != order[None, :])
    highest = jnp.max(jnp.where(usable, similar, -1e30), axis=1)
    scores = jnp.where(jnp.any(usable, axis=1), highest, 0.0)
    total = jnp.sum(jnp.where(valid[:, None], widened, 0.0), axis=0)
    center = total * lax.rsqrt(jnp.mean(total * total) + epsilon)
    return (scores, center)


def shards(embeddings, centroids, cluster, noise_salt):
    rows_dev, feature_dim = embeddings.shape
    cent_dev = centroids.shape[0]
    ny, nz, nx, nc = (lax.axis_size(a) for a in ALL)
    devices = ny * nz * nx * nc
    capacity = max(2, 2 * rows_dev // devices)
    iy, iz, ix, ic = (lax.axis_index(a) for a in ALL)
    me = ((iy * nz + iz) * nx + ix) * nc + ic
    salt_word = noise_salt[0]
    swap = [(i, (i + 1) % nc) for i in range(nc)]
    ring_y = [
        embeddings if s == 0 else lax.ppermute(embeddings, "y", [(i, (i + s) % ny) for i in range(ny)])
        for s in range(ny)
    ]
    group = jnp.concatenate(ring_y + [lax.ppermute(p, "c", swap) for p in ring_y], axis=0)
    piece = lax.all_gather(centroids, ("z", "x"), axis=0, tiled=True)
    src_c = jnp.stack([ic, (ic + nc - 1) % nc])
    src_y = (iy - jnp.arange(ny, dtype=jnp.int32)) % ny
    row_dev = ((src_y[None, :] * nz + iz) * nx + ix) * nc + src_c[:, None]
    group_ids = (row_dev[:, :, None] * rows_dev + jnp.arange(rows_dev, dtype=jnp.int32)).reshape(-1)
    cpos = jnp.arange(nz * nx * cent_dev, dtype=jnp.int32)
    cent_dev_ids = ((iy * nz + cpos // (nx * cent_dev)) * nx + cpos // cent_dev % nx) * nc + ic
    cent_ids = cent_dev_ids * cent_dev + cpos % cent_dev
    noise = gumbel_noise(group_ids[:, None], cent_ids[None, :], salt_word)
    result = score_max(group, piece, noise)
    blocks = result.reshape(nc, ny, rows_dev)
    best = blocks[0, 0]
    for sc in range(nc):
        for sy in range(ny):
            if sc == 0 and sy == 0:
                continue
            perm = [(yy * nc + cc, (yy - sy) % ny * nc + (cc - sc) % nc) for yy in range(ny) for cc in range(nc)]
            best = jnp.maximum(best, lax.ppermute(blocks[sc, sy], ("y", "c"), perm))
    perturbed_max = best
    assigned = cluster[:, 0]
    order = jnp.arange(rows_dev, dtype=jnp.int32)
    same = (assigned[:, None] == assigned[None, :]) & (order[None, :] < order[:, None])
    rank = jnp.sum(same.astype(jnp.int32), axis=1)
    slot = assigned * capacity + rank
    flag_width = 128
    tagged = jnp.concatenate([embeddings, jnp.ones((rows_dev, flag_width), jnp.bfloat16)], axis=1)
    outgoing = jnp.zeros((devices * capacity, feature_dim + flag_width), jnp.bfloat16).at[slot].set(tagged)
    received = lax.all_to_all(
        outgoing.reshape(devices, capacity, feature_dim + flag_width), ALL, split_axis=0, concat_axis=0, tiled=True
    ).reshape(devices * capacity, feature_dim + flag_width)
    members = received[:, :feature_dim]
    valid = received[:, feature_dim] > 0.5
    scores, center = cluster_stats(members, valid)
    returned = lax.all_to_all(
        scores.reshape(devices, capacity), ALL, split_axis=0, concat_axis=0, tiled=True
    )
    dedup_score = returned.reshape(devices * capacity)[slot]
    return (perturbed_max, dedup_score, center[None, :])


def solution(mesh):
    cent_count, rows_count = mesh.devices.shape
    cores = 2
    side = math.isqrt(rows_count // cores)
    view = Mesh(mesh.devices.reshape(cent_count, side, rows_count // cores // side, cores), ALL)
    spec = P(ALL, None)
    in_specs = (spec, spec, spec, P())
    out_specs = (P(ALL), P(ALL), spec)
    return jax.shard_map(shards, mesh=view, in_specs=in_specs, out_specs=out_specs, check_vma=False)
```

```python
import functools
import math

import jax
import jax.numpy as jnp
from jax import lax
from jax.experimental import pallas as pl
from jax.experimental.pallas import tpu as pltpu
from jax.sharding import Mesh
from jax.sharding import PartitionSpec as P

inverse_temp = 3.0
epsilon = 1e-06
ALL = ("y", "z", "x", "c")


def logical_shift(word, amount):
    return lax.shift_right_logical(word, jnp.full(word.shape, amount, jnp.int32))


def gumbel_noise(row_ids, cent_ids, salt_word):
    mixed = row_ids * 1103515245 + cent_ids * 739982445 + salt_word
    mixed = mixed ^ logical_shift(mixed, 16)
    mixed = mixed * 2146121005
    mixed = mixed ^ logical_shift(mixed, 15)
    mixed = mixed * 1759714725
    mixed = mixed ^ logical_shift(mixed, 16)
    low_bits = mixed & 8388607
    uniform = (low_bits.astype(jnp.float32) + 0.5) * (1.0 / 8388608.0)
    return -jnp.log(-jnp.log(uniform))


def gather_kernel(axes, sizes, x_ref, out_ref, send_sem, recv_sem, local_sem):
    n = math.prod(sizes)
    where = {a: lax.axis_index(a) for a in ALL}
    me = 0
    for a, size in zip(axes, sizes):
        me = me * size + where[a]

    def device_of(index):
        coords = dict(where)
        for a, size in reversed(list(zip(axes, sizes))):
            coords[a] = lax.rem(index, size)
            index = index // size
        return tuple(coords[a] for a in ALL)

    peers = [lax.rem(me + k, n) for k in range(n)]
    barrier = pltpu.get_barrier_semaphore()
    for k in range(1, n):
        pl.semaphore_signal(barrier, inc=1, device_id=device_of(peers[k]), device_id_type=pl.DeviceIdType.MESH)
    pl.semaphore_wait(barrier, n - 1)
    local = pltpu.make_async_copy(x_ref, out_ref.at[me], local_sem)
    local.start()
    sends = []
    for k in range(1, n):
        copy = pltpu.make_async_remote_copy(
            src_ref=x_ref,
            dst_ref=out_ref.at[me],
            send_sem=send_sem.at[k],
            recv_sem=recv_sem.at[me],
            device_id=device_of(peers[k]),
            device_id_type=pl.DeviceIdType.MESH,
        )
        copy.start()
        sends.append(copy)
    for k in range(1, n):
        source = lax.rem(me + n - k, n)
        pltpu.make_async_remote_copy(
            src_ref=x_ref,
            dst_ref=out_ref.at[source],
            send_sem=send_sem.at[k],
            recv_sem=recv_sem.at[source],
            device_id=device_of(source),
            device_id_type=pl.DeviceIdType.MESH,
        ).wait_recv()
    for copy in sends:
        copy.wait_send()
    local.wait()


def gather(x, axes, collective_id):
    sizes = tuple(lax.axis_size(a) for a in axes)
    n = math.prod(sizes)
    out = pl.pallas_call(
        functools.partial(gather_kernel, axes, sizes),
        out_shape=jax.ShapeDtypeStruct((n,) + x.shape, x.dtype),
        in_specs=[pl.BlockSpec(memory_space=pl.ANY)],
        out_specs=pl.BlockSpec(memory_space=pl.ANY),
        scratch_shapes=[
            pltpu.SemaphoreType.DMA((n,)),
            pltpu.SemaphoreType.DMA((n,)),
            pltpu.SemaphoreType.DMA,
        ],
        compiler_params=pltpu.CompilerParams(collective_id=collective_id, has_side_effects=True),
    )(x)
    return out.reshape((n * x.shape[0],) + x.shape[1:])


def score_kernel(rows_ref, cents_ref, noise_ref, out_ref):
    scores = lax.dot_general(
        rows_ref[...], cents_ref[...], (((1,), (1,)), ((), ())), preferred_element_type=jnp.float32
    )
    best = jnp.max(inverse_temp * scores + noise_ref[...], axis=1, keepdims=True)

    @pl.when(pl.program_id(1) == 0)
    def _():
        out_ref[...] = best

    @pl.when(pl.program_id(1) > 0)
    def _():
        out_ref[...] = jnp.maximum(out_ref[...], best)


def score_max(rows, cents, noise):
    count, width = rows.shape
    tm = min(1024, count)
    tn = min(512, cents.shape[0])
    out = pl.pallas_call(
        score_kernel,
        out_shape=jax.ShapeDtypeStruct((count, 1), jnp.float32),
        grid=(count // tm, cents.shape[0] // tn),
        in_specs=[
            pl.BlockSpec((tm, width), lambda i, j: (i, 0)),
            pl.BlockSpec((tn, width), lambda i, j: (j, 0)),
            pl.BlockSpec((tm, tn), lambda i, j: (i, j)),
        ],
        out_specs=pl.BlockSpec((tm, 1), lambda i, j: (i, 0)),
        compiler_params=pltpu.CompilerParams(dimension_semantics=("parallel", "arbitrary")),
    )(rows, cents, noise)
    return out[:, 0]


def cluster_stats(members, valid):
    feature_dim = members.shape[1]
    widened = members.astype(jnp.float32)
    scale = lax.rsqrt(jnp.mean(widened * widened, axis=1) + epsilon)
    gram = lax.dot_general(
        members, members, (((1,), (1,)), ((), ())), preferred_element_type=jnp.float32
    )
    similar = gram * scale[:, None] * scale[None, :] * (1.0 / math.sqrt(feature_dim))
    order = jnp.arange(members.shape[0], dtype=jnp.int32)
    usable = valid[None, :] & (order[:, None] != order[None, :])
    highest = jnp.max(jnp.where(usable, similar, -1e30), axis=1)
    scores = jnp.where(jnp.any(usable, axis=1), highest, 0.0)
    total = jnp.sum(jnp.where(valid[:, None], widened, 0.0), axis=0)
    center = total * lax.rsqrt(jnp.mean(total * total) + epsilon)
    return (scores, center)


def shards(embeddings, centroids, cluster, noise_salt):
    rows_dev, feature_dim = embeddings.shape
    cent_dev = centroids.shape[0]
    ny, nz, nx, nc = (lax.axis_size(a) for a in ALL)
    devices = ny * nz * nx * nc
    capacity = max(2, 2 * rows_dev // devices)
    iy, iz, ix, ic = (lax.axis_index(a) for a in ALL)
    me = ((iy * nz + iz) * nx + ix) * nc + ic
    salt_word = noise_salt[0]
    swap = [(i, (i + 1) % nc) for i in range(nc)]
    ring_y = [
        embeddings if s == 0 else lax.ppermute(embeddings, "y", [(i, (i + s) % ny) for i in range(ny)])
        for s in range(ny)
    ]
    group = jnp.concatenate(ring_y + [lax.ppermute(p, "c", swap) for p in ring_y], axis=0)
    piece = lax.all_gather(centroids, ("z", "x"), axis=0, tiled=True)
    src_c = jnp.stack([ic, (ic + nc - 1) % nc])
    src_y = (iy - jnp.arange(ny, dtype=jnp.int32)) % ny
    row_dev = ((src_y[None, :] * nz + iz) * nx + ix) * nc + src_c[:, None]
    group_ids = (row_dev[:, :, None] * rows_dev + jnp.arange(rows_dev, dtype=jnp.int32)).reshape(-1)
    cpos = jnp.arange(nz * nx * cent_dev, dtype=jnp.int32)
    cent_dev_ids = ((iy * nz + cpos // (nx * cent_dev)) * nx + cpos // cent_dev % nx) * nc + ic
    cent_ids = cent_dev_ids * cent_dev + cpos % cent_dev
    noise = gumbel_noise(group_ids[:, None], cent_ids[None, :], salt_word)
    result = score_max(group, piece, noise)
    owner = jnp.arange(ny * nc, dtype=jnp.int32)
    picked = (ic - owner % nc) % nc * ny + (iy - owner // nc) % ny
    outbound = jnp.take(result.reshape(nc * ny, rows_dev), picked, axis=0)
    inbound = lax.all_to_all(outbound, ("y", "c"), split_axis=0, concat_axis=0, tiled=True)
    perturbed_max = jnp.max(inbound, axis=0)
    assigned = cluster[:, 0]
    order = jnp.arange(rows_dev, dtype=jnp.int32)
    same = (assigned[:, None] == assigned[None, :]) & (order[None, :] < order[:, None])
    rank = jnp.sum(same.astype(jnp.int32), axis=1)
    slot = assigned * capacity + rank
    flag_width = 128
    tagged = jnp.concatenate([embeddings, jnp.ones((rows_dev, flag_width), jnp.bfloat16)], axis=1)
    outgoing = jnp.zeros((devices * capacity, feature_dim + flag_width), jnp.bfloat16).at[slot].set(tagged)
    received = lax.all_to_all(
        outgoing.reshape(devices, capacity, feature_dim + flag_width), ALL, split_axis=0, concat_axis=0, tiled=True
    ).reshape(devices * capacity, feature_dim + flag_width)
    members = received[:, :feature_dim]
    valid = received[:, feature_dim] > 0.5
    scores, center = cluster_stats(members, valid)
    returned = lax.all_to_all(
        scores.reshape(devices, capacity), ALL, split_axis=0, concat_axis=0, tiled=True
    )
    dedup_score = returned.reshape(devices * capacity)[slot]
    return (perturbed_max, dedup_score, center[None, :])


def solution(mesh):
    cent_count, rows_count = mesh.devices.shape
    cores = 2
    side = math.isqrt(rows_count // cores)
    view = Mesh(mesh.devices.reshape(cent_count, side, rows_count // cores // side, cores), ALL)
    spec = P(ALL, None)
    in_specs = (spec, spec, spec, P())
    out_specs = (P(ALL), P(ALL), spec)
    return jax.shard_map(shards, mesh=view, in_specs=in_specs, out_specs=out_specs, check_vma=False)
```

```python
import functools
import math

import jax
import jax.numpy as jnp
from jax import lax
from jax.experimental import pallas as pl
from jax.experimental.pallas import tpu as pltpu
from jax.sharding import Mesh
from jax.sharding import PartitionSpec as P

inverse_temp = 3.0
epsilon = 1e-06
ALL = ("y", "z", "x", "c")


def logical_shift(word, amount):
    return lax.shift_right_logical(word, jnp.full(word.shape, amount, jnp.int32))


def gumbel_noise(row_ids, cent_ids, salt_word):
    mixed = row_ids * 1103515245 + cent_ids * 739982445 + salt_word
    mixed = mixed ^ logical_shift(mixed, 16)
    mixed = mixed * 2146121005
    mixed = mixed ^ logical_shift(mixed, 15)
    mixed = mixed * 1759714725
    mixed = mixed ^ logical_shift(mixed, 16)
    low_bits = mixed & 8388607
    uniform = (low_bits.astype(jnp.float32) + 0.5) * (1.0 / 8388608.0)
    return -jnp.log(-jnp.log(uniform))


def gather_kernel(axes, sizes, x_ref, out_ref, send_sem, recv_sem, local_sem):
    n = math.prod(sizes)
    where = {a: lax.axis_index(a) for a in ALL}
    me = 0
    for a, size in zip(axes, sizes):
        me = me * size + where[a]

    def device_of(index):
        coords = dict(where)
        for a, size in reversed(list(zip(axes, sizes))):
            coords[a] = lax.rem(index, size)
            index = index // size
        return tuple(coords[a] for a in ALL)

    peers = [lax.rem(me + k, n) for k in range(n)]
    barrier = pltpu.get_barrier_semaphore()
    for k in range(1, n):
        pl.semaphore_signal(barrier, inc=1, device_id=device_of(peers[k]), device_id_type=pl.DeviceIdType.MESH)
    pl.semaphore_wait(barrier, n - 1)
    local = pltpu.make_async_copy(x_ref, out_ref.at[me], local_sem)
    local.start()
    sends = []
    for k in range(1, n):
        copy = pltpu.make_async_remote_copy(
            src_ref=x_ref,
            dst_ref=out_ref.at[me],
            send_sem=send_sem.at[k],
            recv_sem=recv_sem.at[me],
            device_id=device_of(peers[k]),
            device_id_type=pl.DeviceIdType.MESH,
        )
        copy.start()
        sends.append(copy)
    for k in range(1, n):
        source = lax.rem(me + n - k, n)
        pltpu.make_async_remote_copy(
            src_ref=x_ref,
            dst_ref=out_ref.at[source],
            send_sem=send_sem.at[k],
            recv_sem=recv_sem.at[source],
            device_id=device_of(source),
            device_id_type=pl.DeviceIdType.MESH,
        ).wait_recv()
    for copy in sends:
        copy.wait_send()
    local.wait()


def gather(x, axes, collective_id):
    sizes = tuple(lax.axis_size(a) for a in axes)
    n = math.prod(sizes)
    out = pl.pallas_call(
        functools.partial(gather_kernel, axes, sizes),
        out_shape=jax.ShapeDtypeStruct((n,) + x.shape, x.dtype),
        in_specs=[pl.BlockSpec(memory_space=pl.ANY)],
        out_specs=pl.BlockSpec(memory_space=pl.ANY),
        scratch_shapes=[
            pltpu.SemaphoreType.DMA((n,)),
            pltpu.SemaphoreType.DMA((n,)),
            pltpu.SemaphoreType.DMA,
        ],
        compiler_params=pltpu.CompilerParams(collective_id=collective_id, has_side_effects=True),
    )(x)
    return out.reshape((n * x.shape[0],) + x.shape[1:])


def score_kernel(rows_ref, cents_ref, noise_ref, out_ref):
    scores = lax.dot_general(
        rows_ref[...], cents_ref[...], (((1,), (1,)), ((), ())), preferred_element_type=jnp.float32
    )
    best = jnp.max(inverse_temp * scores + noise_ref[...], axis=1, keepdims=True)

    @pl.when(pl.program_id(1) == 0)
    def _():
        out_ref[...] = best

    @pl.when(pl.program_id(1) > 0)
    def _():
        out_ref[...] = jnp.maximum(out_ref[...], best)


def score_max(rows, cents, noise):
    count, width = rows.shape
    tm = min(1024, count)
    tn = min(512, cents.shape[0])
    out = pl.pallas_call(
        score_kernel,
        out_shape=jax.ShapeDtypeStruct((count, 1), jnp.float32),
        grid=(count // tm, cents.shape[0] // tn),
        in_specs=[
            pl.BlockSpec((tm, width), lambda i, j: (i, 0)),
            pl.BlockSpec((tn, width), lambda i, j: (j, 0)),
            pl.BlockSpec((tm, tn), lambda i, j: (i, j)),
        ],
        out_specs=pl.BlockSpec((tm, 1), lambda i, j: (i, 0)),
        compiler_params=pltpu.CompilerParams(dimension_semantics=("parallel", "arbitrary")),
    )(rows, cents, noise)
    return out[:, 0]


def cluster_stats(members, valid):
    feature_dim = members.shape[1]
    widened = members.astype(jnp.float32)
    scale = lax.rsqrt(jnp.mean(widened * widened, axis=1) + epsilon)
    gram = lax.dot_general(
        members, members, (((1,), (1,)), ((), ())), preferred_element_type=jnp.float32
    )
    similar = gram * scale[:, None] * scale[None, :] * (1.0 / math.sqrt(feature_dim))
    order = jnp.arange(members.shape[0], dtype=jnp.int32)
    usable = valid[None, :] & (order[:, None] != order[None, :])
    highest = jnp.max(jnp.where(usable, similar, -1e30), axis=1)
    scores = jnp.where(jnp.any(usable, axis=1), highest, 0.0)
    total = jnp.sum(jnp.where(valid[:, None], widened, 0.0), axis=0)
    center = total * lax.rsqrt(jnp.mean(total * total) + epsilon)
    return (scores, center)


def shards(embeddings, centroids, cluster, noise_salt):
    rows_dev, feature_dim = embeddings.shape
    cent_dev = centroids.shape[0]
    ny, nz, nx, nc = (lax.axis_size(a) for a in ALL)
    devices = ny * nz * nx * nc
    capacity = max(2, 2 * rows_dev // devices)
    iy, iz, ix, ic = (lax.axis_index(a) for a in ALL)
    me = ((iy * nz + iz) * nx + ix) * nc + ic
    salt_word = noise_salt[0]
    swap = [(i, (i + 1) % nc) for i in range(nc)]
    ring_y = [
        embeddings if s == 0 else lax.ppermute(embeddings, "y", [(i, (i + s) % ny) for i in range(ny)])
        for s in range(ny)
    ]
    group = jnp.concatenate(ring_y + [lax.ppermute(p, "c", swap) for p in ring_y], axis=0)
    piece = lax.all_gather(centroids, ("z", "x"), axis=0, tiled=True)
    src_c = jnp.stack([ic, (ic + nc - 1) % nc])
    src_y = (iy - jnp.arange(ny, dtype=jnp.int32)) % ny
    row_dev = ((src_y[None, :] * nz + iz) * nx + ix) * nc + src_c[:, None]
    group_ids = (row_dev[:, :, None] * rows_dev + jnp.arange(rows_dev, dtype=jnp.int32)).reshape(-1)
    cpos = jnp.arange(nz * nx * cent_dev, dtype=jnp.int32)
    cent_dev_ids = ((iy * nz + cpos // (nx * cent_dev)) * nx + cpos // cent_dev % nx) * nc + ic
    cent_ids = cent_dev_ids * cent_dev + cpos % cent_dev
    assigned = cluster[:, 0]
    order = jnp.arange(rows_dev, dtype=jnp.int32)
    same = (assigned[:, None] == assigned[None, :]) & (order[None, :] < order[:, None])
    rank = jnp.sum(same.astype(jnp.int32), axis=1)
    slot = assigned * capacity + rank
    flag_width = 128
    tagged = jnp.concatenate([embeddings, jnp.ones((rows_dev, flag_width), jnp.bfloat16)], axis=1)
    outgoing = jnp.zeros((devices * capacity, feature_dim + flag_width), jnp.bfloat16).at[slot].set(tagged)
    outgoing, piece = lax.optimization_barrier((outgoing, piece))
    received = lax.all_to_all(
        outgoing.reshape(devices, capacity, feature_dim + flag_width), ALL, split_axis=0, concat_axis=0, tiled=True
    ).reshape(devices * capacity, feature_dim + flag_width)
    members = received[:, :feature_dim]
    valid = received[:, feature_dim] > 0.5
    noise = gumbel_noise(group_ids[:, None], cent_ids[None, :], salt_word)
    result = score_max(group, piece, noise)
    owner = jnp.arange(ny * nc, dtype=jnp.int32)
    picked = (ic - owner % nc) % nc * ny + (iy - owner // nc) % ny
    outbound = jnp.take(result.reshape(nc * ny, rows_dev), picked, axis=0)
    inbound = lax.all_to_all(outbound, ("y", "c"), split_axis=0, concat_axis=0, tiled=True)
    perturbed_max = jnp.max(inbound, axis=0)
    scores, center = cluster_stats(members, valid)
    returned = lax.all_to_all(
        scores.reshape(devices, capacity), ALL, split_axis=0, concat_axis=0, tiled=True
    )
    dedup_score = returned.reshape(devices * capacity)[slot]
    return (perturbed_max, dedup_score, center[None, :])


def solution(mesh):
    cent_count, rows_count = mesh.devices.shape
    cores = 2
    side = math.isqrt(rows_count // cores)
    view = Mesh(mesh.devices.reshape(cent_count, side, rows_count // cores // side, cores), ALL)
    spec = P(ALL, None)
    in_specs = (spec, spec, spec, P())
    out_specs = (P(ALL), P(ALL), spec)
    return jax.shard_map(shards, mesh=view, in_specs=in_specs, out_specs=out_specs, check_vma=False)
```

```python
import functools
import math

import jax
import jax.numpy as jnp
from jax import lax
from jax.experimental import pallas as pl
from jax.experimental.pallas import tpu as pltpu
from jax.sharding import Mesh
from jax.sharding import PartitionSpec as P

inverse_temp = 3.0
epsilon = 1e-06
ALL = ("y", "z", "x", "c")


def logical_shift(word, amount):
    return lax.shift_right_logical(word, jnp.full(word.shape, amount, jnp.int32))


def gumbel_noise(row_ids, cent_ids, salt_word):
    mixed = row_ids * 1103515245 + cent_ids * 739982445 + salt_word
    mixed = mixed ^ logical_shift(mixed, 16)
    mixed = mixed * 2146121005
    mixed = mixed ^ logical_shift(mixed, 15)
    mixed = mixed * 1759714725
    mixed = mixed ^ logical_shift(mixed, 16)
    low_bits = mixed & 8388607
    uniform = (low_bits.astype(jnp.float32) + 0.5) * (1.0 / 8388608.0)
    return -jnp.log(-jnp.log(uniform))


def gather_kernel(axes, sizes, x_ref, out_ref, send_sem, recv_sem, local_sem):
    n = math.prod(sizes)
    where = {a: lax.axis_index(a) for a in ALL}
    me = 0
    for a, size in zip(axes, sizes):
        me = me * size + where[a]

    def device_of(index):
        coords = dict(where)
        for a, size in reversed(list(zip(axes, sizes))):
            coords[a] = lax.rem(index, size)
            index = index // size
        return tuple(coords[a] for a in ALL)

    peers = [lax.rem(me + k, n) for k in range(n)]
    barrier = pltpu.get_barrier_semaphore()
    for k in range(1, n):
        pl.semaphore_signal(barrier, inc=1, device_id=device_of(peers[k]), device_id_type=pl.DeviceIdType.MESH)
    pl.semaphore_wait(barrier, n - 1)
    local = pltpu.make_async_copy(x_ref, out_ref.at[me], local_sem)
    local.start()
    sends = []
    for k in range(1, n):
        copy = pltpu.make_async_remote_copy(
            src_ref=x_ref,
            dst_ref=out_ref.at[me],
            send_sem=send_sem.at[k],
            recv_sem=recv_sem.at[me],
            device_id=device_of(peers[k]),
            device_id_type=pl.DeviceIdType.MESH,
        )
        copy.start()
        sends.append(copy)
    for k in range(1, n):
        source = lax.rem(me + n - k, n)
        pltpu.make_async_remote_copy(
            src_ref=x_ref,
            dst_ref=out_ref.at[source],
            send_sem=send_sem.at[k],
            recv_sem=recv_sem.at[source],
            device_id=device_of(source),
            device_id_type=pl.DeviceIdType.MESH,
        ).wait_recv()
    for copy in sends:
        copy.wait_send()
    local.wait()


def gather(x, axes, collective_id):
    sizes = tuple(lax.axis_size(a) for a in axes)
    n = math.prod(sizes)
    out = pl.pallas_call(
        functools.partial(gather_kernel, axes, sizes),
        out_shape=jax.ShapeDtypeStruct((n,) + x.shape, x.dtype),
        in_specs=[pl.BlockSpec(memory_space=pl.ANY)],
        out_specs=pl.BlockSpec(memory_space=pl.ANY),
        scratch_shapes=[
            pltpu.SemaphoreType.DMA((n,)),
            pltpu.SemaphoreType.DMA((n,)),
            pltpu.SemaphoreType.DMA,
        ],
        compiler_params=pltpu.CompilerParams(collective_id=collective_id, has_side_effects=True),
    )(x)
    return out.reshape((n * x.shape[0],) + x.shape[1:])


def score_kernel(rows_ref, cents_ref, noise_ref, out_ref, acc_ref):
    scores = lax.dot_general(
        rows_ref[...], cents_ref[...], (((1,), (1,)), ((), ())), preferred_element_type=jnp.float32
    )
    perturbed = inverse_temp * scores + noise_ref[...]
    lanes = acc_ref.shape[1]
    folded = perturbed[:, :lanes]
    for k in range(1, perturbed.shape[1] // lanes):
        folded = jnp.maximum(folded, perturbed[:, k * lanes:(k + 1) * lanes])
    step = pl.program_id(1)

    @pl.when(step == 0)
    def _():
        acc_ref[...] = folded

    @pl.when(step > 0)
    def _():
        acc_ref[...] = jnp.maximum(acc_ref[...], folded)

    @pl.when(step == pl.num_programs(1) - 1)
    def _():
        out_ref[...] = jnp.max(acc_ref[...], axis=1, keepdims=True)


def score_max(rows, cents, noise):
    count, width = rows.shape
    tm = min(1024, count)
    tn = min(512, cents.shape[0])
    out = pl.pallas_call(
        score_kernel,
        out_shape=jax.ShapeDtypeStruct((count, 1), jnp.float32),
        grid=(count // tm, cents.shape[0] // tn),
        in_specs=[
            pl.BlockSpec((tm, width), lambda i, j: (i, 0)),
            pl.BlockSpec((tn, width), lambda i, j: (j, 0)),
            pl.BlockSpec((tm, tn), lambda i, j: (i, j)),
        ],
        out_specs=pl.BlockSpec((tm, 1), lambda i, j: (i, 0)),
        scratch_shapes=[pltpu.VMEM((tm, 128), jnp.float32)],
        compiler_params=pltpu.CompilerParams(dimension_semantics=("parallel", "arbitrary")),
    )(rows, cents, noise)
    return out[:, 0]


def cluster_stats(members, valid):
    feature_dim = members.shape[1]
    widened = members.astype(jnp.float32)
    scale = lax.rsqrt(jnp.mean(widened * widened, axis=1) + epsilon)
    gram = lax.dot_general(
        members, members, (((1,), (1,)), ((), ())), preferred_element_type=jnp.float32
    )
    similar = gram * scale[:, None] * scale[None, :] * (1.0 / math.sqrt(feature_dim))
    order = jnp.arange(members.shape[0], dtype=jnp.int32)
    usable = valid[None, :] & (order[:, None] != order[None, :])
    highest = jnp.max(jnp.where(usable, similar, -1e30), axis=1)
    scores = jnp.where(jnp.any(usable, axis=1), highest, 0.0)
    total = jnp.sum(jnp.where(valid[:, None], widened, 0.0), axis=0)
    center = total * lax.rsqrt(jnp.mean(total * total) + epsilon)
    return (scores, center)


def shards(embeddings, centroids, cluster, noise_salt):
    rows_dev, feature_dim = embeddings.shape
    cent_dev = centroids.shape[0]
    ny, nz, nx, nc = (lax.axis_size(a) for a in ALL)
    devices = ny * nz * nx * nc
    capacity = max(2, 2 * rows_dev // devices)
    iy, iz, ix, ic = (lax.axis_index(a) for a in ALL)
    me = ((iy * nz + iz) * nx + ix) * nc + ic
    salt_word = noise_salt[0]
    swap = [(i, (i + 1) % nc) for i in range(nc)]
    ring_y = [
        embeddings if s == 0 else lax.ppermute(embeddings, "y", [(i, (i + s) % ny) for i in range(ny)])
        for s in range(ny)
    ]
    group = jnp.concatenate(ring_y + [lax.ppermute(p, "c", swap) for p in ring_y], axis=0)
    piece = lax.all_gather(centroids, ("z", "x"), axis=0, tiled=True)
    src_c = jnp.stack([ic, (ic + nc - 1) % nc])
    src_y = (iy - jnp.arange(ny, dtype=jnp.int32)) % ny
    row_dev = ((src_y[None, :] * nz + iz) * nx + ix) * nc + src_c[:, None]
    group_ids = (row_dev[:, :, None] * rows_dev + jnp.arange(rows_dev, dtype=jnp.int32)).reshape(-1)
    cpos = jnp.arange(nz * nx * cent_dev, dtype=jnp.int32)
    cent_dev_ids = ((iy * nz + cpos // (nx * cent_dev)) * nx + cpos // cent_dev % nx) * nc + ic
    cent_ids = cent_dev_ids * cent_dev + cpos % cent_dev
    noise = gumbel_noise(group_ids[:, None], cent_ids[None, :], salt_word)
    result = score_max(group, piece, noise)
    owner = jnp.arange(ny * nc, dtype=jnp.int32)
    picked = (ic - owner % nc) % nc * ny + (iy - owner // nc) % ny
    outbound = jnp.take(result.reshape(nc * ny, rows_dev), picked, axis=0)
    inbound = lax.all_to_all(outbound, ("y", "c"), split_axis=0, concat_axis=0, tiled=True)
    perturbed_max = jnp.max(inbound, axis=0)
    assigned = cluster[:, 0]
    order = jnp.arange(rows_dev, dtype=jnp.int32)
    same = (assigned[:, None] == assigned[None, :]) & (order[None, :] < order[:, None])
    rank = jnp.sum(same.astype(jnp.int32), axis=1)
    slot = assigned * capacity + rank
    flag_width = 128
    tagged = jnp.concatenate([embeddings, jnp.ones((rows_dev, flag_width), jnp.bfloat16)], axis=1)
    outgoing = jnp.zeros((devices * capacity, feature_dim + flag_width), jnp.bfloat16).at[slot].set(tagged)
    received = lax.all_to_all(
        outgoing.reshape(devices, capacity, feature_dim + flag_width), ALL, split_axis=0, concat_axis=0, tiled=True
    ).reshape(devices * capacity, feature_dim + flag_width)
    members = received[:, :feature_dim]
    valid = received[:, feature_dim] > 0.5
    scores, center = cluster_stats(members, valid)
    returned = lax.all_to_all(
        scores.reshape(devices, capacity), ALL, split_axis=0, concat_axis=0, tiled=True
    )
    dedup_score = returned.reshape(devices * capacity)[slot]
    return (perturbed_max, dedup_score, center[None, :])


def solution(mesh):
    cent_count, rows_count = mesh.devices.shape
    cores = 2
    side = math.isqrt(rows_count // cores)
    view = Mesh(mesh.devices.reshape(cent_count, side, rows_count // cores // side, cores), ALL)
    spec = P(ALL, None)
    in_specs = (spec, spec, spec, P())
    out_specs = (P(ALL), P(ALL), spec)
    return jax.shard_map(shards, mesh=view, in_specs=in_specs, out_specs=out_specs, check_vma=False)
```

```python
import functools
import math

import jax
import jax.numpy as jnp
from jax import lax
from jax.experimental import pallas as pl
from jax.experimental.pallas import tpu as pltpu
from jax.sharding import Mesh
from jax.sharding import PartitionSpec as P

inverse_temp = 3.0
epsilon = 1e-06
ALL = ("y", "z", "x", "c")


def logical_shift(word, amount):
    return lax.shift_right_logical(word, jnp.full(word.shape, amount, jnp.int32))


def gumbel_noise(row_ids, cent_ids, salt_word):
    mixed = row_ids * 1103515245 + cent_ids * 739982445 + salt_word
    mixed = mixed ^ logical_shift(mixed, 16)
    mixed = mixed * 2146121005
    mixed = mixed ^ logical_shift(mixed, 15)
    mixed = mixed * 1759714725
    mixed = mixed ^ logical_shift(mixed, 16)
    low_bits = mixed & 8388607
    uniform = (low_bits.astype(jnp.float32) + 0.5) * (1.0 / 8388608.0)
    return -jnp.log(-jnp.log(uniform))


def gather_kernel(axes, sizes, x_ref, out_ref, send_sem, recv_sem, local_sem):
    n = math.prod(sizes)
    where = {a: lax.axis_index(a) for a in ALL}
    me = 0
    for a, size in zip(axes, sizes):
        me = me * size + where[a]

    def device_of(index):
        coords = dict(where)
        for a, size in reversed(list(zip(axes, sizes))):
            coords[a] = lax.rem(index, size)
            index = index // size
        return tuple(coords[a] for a in ALL)

    peers = [lax.rem(me + k, n) for k in range(n)]
    barrier = pltpu.get_barrier_semaphore()
    for k in range(1, n):
        pl.semaphore_signal(barrier, inc=1, device_id=device_of(peers[k]), device_id_type=pl.DeviceIdType.MESH)
    pl.semaphore_wait(barrier, n - 1)
    local = pltpu.make_async_copy(x_ref, out_ref.at[me], local_sem)
    local.start()
    sends = []
    for k in range(1, n):
        copy = pltpu.make_async_remote_copy(
            src_ref=x_ref,
            dst_ref=out_ref.at[me],
            send_sem=send_sem.at[k],
            recv_sem=recv_sem.at[me],
            device_id=device_of(peers[k]),
            device_id_type=pl.DeviceIdType.MESH,
        )
        copy.start()
        sends.append(copy)
    for k in range(1, n):
        source = lax.rem(me + n - k, n)
        pltpu.make_async_remote_copy(
            src_ref=x_ref,
            dst_ref=out_ref.at[source],
            send_sem=send_sem.at[k],
            recv_sem=recv_sem.at[source],
            device_id=device_of(source),
            device_id_type=pl.DeviceIdType.MESH,
        ).wait_recv()
    for copy in sends:
        copy.wait_send()
    local.wait()


def gather(x, axes, collective_id):
    sizes = tuple(lax.axis_size(a) for a in axes)
    n = math.prod(sizes)
    out = pl.pallas_call(
        functools.partial(gather_kernel, axes, sizes),
        out_shape=jax.ShapeDtypeStruct((n,) + x.shape, x.dtype),
        in_specs=[pl.BlockSpec(memory_space=pl.ANY)],
        out_specs=pl.BlockSpec(memory_space=pl.ANY),
        scratch_shapes=[
            pltpu.SemaphoreType.DMA((n,)),
            pltpu.SemaphoreType.DMA((n,)),
            pltpu.SemaphoreType.DMA,
        ],
        compiler_params=pltpu.CompilerParams(collective_id=collective_id, has_side_effects=True),
    )(x)
    return out.reshape((n * x.shape[0],) + x.shape[1:])


def score_kernel(rows_ref, cents_ref, noise_ref, out_ref, acc_ref):
    scores = lax.dot_general(
        rows_ref[...], cents_ref[...], (((1,), (1,)), ((), ())), preferred_element_type=jnp.float32
    )
    perturbed = inverse_temp * scores + noise_ref[...]
    lanes = acc_ref.shape[1]
    folded = perturbed[:, :lanes]
    for k in range(1, perturbed.shape[1] // lanes):
        folded = jnp.maximum(folded, perturbed[:, k * lanes:(k + 1) * lanes])
    step = pl.program_id(1)

    @pl.when(step == 0)
    def _():
        acc_ref[...] = folded

    @pl.when(step > 0)
    def _():
        acc_ref[...] = jnp.maximum(acc_ref[...], folded)

    @pl.when(step == pl.num_programs(1) - 1)
    def _():
        out_ref[...] = jnp.max(acc_ref[...], axis=1, keepdims=True)


def score_max(rows, cents, noise):
    count, width = rows.shape
    tm = min(1024, count)
    tn = min(512, cents.shape[0])
    out = pl.pallas_call(
        score_kernel,
        out_shape=jax.ShapeDtypeStruct((count, 1), jnp.float32),
        grid=(count // tm, cents.shape[0] // tn),
        in_specs=[
            pl.BlockSpec((tm, width), lambda i, j: (i, 0)),
            pl.BlockSpec((tn, width), lambda i, j: (j, 0)),
            pl.BlockSpec((tm, tn), lambda i, j: (i, j)),
        ],
        out_specs=pl.BlockSpec((tm, 1), lambda i, j: (i, 0)),
        scratch_shapes=[pltpu.VMEM((tm, 128), jnp.float32)],
        compiler_params=pltpu.CompilerParams(dimension_semantics=("parallel", "arbitrary")),
    )(rows, cents, noise)
    return out[:, 0]


def cluster_stats(members, valid):
    feature_dim = members.shape[1]
    widened = members.astype(jnp.float32)
    scale = lax.rsqrt(jnp.mean(widened * widened, axis=1) + epsilon)
    gram = lax.dot_general(
        members, members, (((1,), (1,)), ((), ())), preferred_element_type=jnp.float32
    )
    similar = gram * scale[:, None] * scale[None, :] * (1.0 / math.sqrt(feature_dim))
    order = jnp.arange(members.shape[0], dtype=jnp.int32)
    usable = valid[None, :] & (order[:, None] != order[None, :])
    highest = jnp.max(jnp.where(usable, similar, -1e30), axis=1)
    scores = jnp.where(jnp.any(usable, axis=1), highest, 0.0)
    total = jnp.sum(jnp.where(valid[:, None], widened, 0.0), axis=0)
    center = total * lax.rsqrt(jnp.mean(total * total) + epsilon)
    return (scores, center)


def shards(embeddings, centroids, cluster, noise_salt):
    rows_dev, feature_dim = embeddings.shape
    cent_dev = centroids.shape[0]
    ny, nz, nx, nc = (lax.axis_size(a) for a in ALL)
    devices = ny * nz * nx * nc
    capacity = max(2, 2 * rows_dev // devices)
    iy, iz, ix, ic = (lax.axis_index(a) for a in ALL)
    me = ((iy * nz + iz) * nx + ix) * nc + ic
    salt_word = noise_salt[0]
    swap = [(i, (i + 1) % nc) for i in range(nc)]
    ring_y = [
        embeddings if s == 0 else lax.ppermute(embeddings, "y", [(i, (i + s) % ny) for i in range(ny)])
        for s in range(ny)
    ]
    group = jnp.concatenate(ring_y + [lax.ppermute(p, "c", swap) for p in ring_y], axis=0)
    piece = lax.all_gather(centroids, ("z", "x"), axis=0, tiled=True)
    src_c = jnp.stack([ic, (ic + nc - 1) % nc])
    src_y = (iy - jnp.arange(ny, dtype=jnp.int32)) % ny
    row_dev = ((src_y[None, :] * nz + iz) * nx + ix) * nc + src_c[:, None]
    group_ids = (row_dev[:, :, None] * rows_dev + jnp.arange(rows_dev, dtype=jnp.int32)).reshape(-1)
    cpos = jnp.arange(nz * nx * cent_dev, dtype=jnp.int32)
    cent_dev_ids = ((iy * nz + cpos // (nx * cent_dev)) * nx + cpos // cent_dev % nx) * nc + ic
    cent_ids = cent_dev_ids * cent_dev + cpos % cent_dev
    assigned = cluster[:, 0]
    order = jnp.arange(rows_dev, dtype=jnp.int32)
    same = (assigned[:, None] == assigned[None, :]) & (order[None, :] < order[:, None])
    rank = jnp.sum(same.astype(jnp.int32), axis=1)
    slot = assigned * capacity + rank
    flag_width = 128
    tagged = jnp.concatenate([embeddings, jnp.ones((rows_dev, flag_width), jnp.bfloat16)], axis=1)
    outgoing = jnp.zeros((devices * capacity, feature_dim + flag_width), jnp.bfloat16).at[slot].set(tagged)
    outgoing, piece = lax.optimization_barrier((outgoing, piece))
    received = lax.all_to_all(
        outgoing.reshape(devices, capacity, feature_dim + flag_width), ALL, split_axis=0, concat_axis=0, tiled=True
    ).reshape(devices * capacity, feature_dim + flag_width)
    members = received[:, :feature_dim]
    valid = received[:, feature_dim] > 0.5
    noise = gumbel_noise(group_ids[:, None], cent_ids[None, :], salt_word)
    half = group.shape[0] // 2
    first = score_max(group[:half], piece, noise[:half])
    first, received = lax.optimization_barrier((first, received))
    result = jnp.concatenate([first, score_max(group[half:], piece, noise[half:])])
    owner = jnp.arange(ny * nc, dtype=jnp.int32)
    picked = (ic - owner % nc) % nc * ny + (iy - owner // nc) % ny
    outbound = jnp.take(result.reshape(nc * ny, rows_dev), picked, axis=0)
    inbound = lax.all_to_all(outbound, ("y", "c"), split_axis=0, concat_axis=0, tiled=True)
    perturbed_max = jnp.max(inbound, axis=0)
    scores, center = cluster_stats(members, valid)
    returned = lax.all_to_all(
        scores.reshape(devices, capacity), ALL, split_axis=0, concat_axis=0, tiled=True
    )
    dedup_score = returned.reshape(devices * capacity)[slot]
    return (perturbed_max, dedup_score, center[None, :])


def solution(mesh):
    cent_count, rows_count = mesh.devices.shape
    cores = 2
    side = math.isqrt(rows_count // cores)
    view = Mesh(mesh.devices.reshape(cent_count, side, rows_count // cores // side, cores), ALL)
    spec = P(ALL, None)
    in_specs = (spec, spec, spec, P())
    out_specs = (P(ALL), P(ALL), spec)
    return jax.shard_map(shards, mesh=view, in_specs=in_specs, out_specs=out_specs, check_vma=False)
```

```python
import functools
import math

import jax
import jax.numpy as jnp
from jax import lax
from jax.experimental import pallas as pl
from jax.experimental.pallas import tpu as pltpu
from jax.sharding import Mesh
from jax.sharding import PartitionSpec as P

inverse_temp = 3.0
epsilon = 1e-06
ALL = ("y", "z", "x", "c")


def logical_shift(word, amount):
    return lax.shift_right_logical(word, jnp.full(word.shape, amount, jnp.int32))


def gumbel_noise(row_ids, cent_ids, salt_word):
    mixed = row_ids * 1103515245 + cent_ids * 739982445 + salt_word
    mixed = mixed ^ logical_shift(mixed, 16)
    mixed = mixed * 2146121005
    mixed = mixed ^ logical_shift(mixed, 15)
    mixed = mixed * 1759714725
    mixed = mixed ^ logical_shift(mixed, 16)
    low_bits = mixed & 8388607
    uniform = (low_bits.astype(jnp.float32) + 0.5) * (1.0 / 8388608.0)
    return -jnp.log(-jnp.log(uniform))


def gather_kernel(axes, sizes, x_ref, out_ref, send_sem, recv_sem, local_sem):
    n = math.prod(sizes)
    where = {a: lax.axis_index(a) for a in ALL}
    me = 0
    for a, size in zip(axes, sizes):
        me = me * size + where[a]

    def device_of(index):
        coords = dict(where)
        for a, size in reversed(list(zip(axes, sizes))):
            coords[a] = lax.rem(index, size)
            index = index // size
        return tuple(coords[a] for a in ALL)

    peers = [lax.rem(me + k, n) for k in range(n)]
    barrier = pltpu.get_barrier_semaphore()
    for k in range(1, n):
        pl.semaphore_signal(barrier, inc=1, device_id=device_of(peers[k]), device_id_type=pl.DeviceIdType.MESH)
    pl.semaphore_wait(barrier, n - 1)
    local = pltpu.make_async_copy(x_ref, out_ref.at[me], local_sem)
    local.start()
    sends = []
    for k in range(1, n):
        copy = pltpu.make_async_remote_copy(
            src_ref=x_ref,
            dst_ref=out_ref.at[me],
            send_sem=send_sem.at[k],
            recv_sem=recv_sem.at[me],
            device_id=device_of(peers[k]),
            device_id_type=pl.DeviceIdType.MESH,
        )
        copy.start()
        sends.append(copy)
    for k in range(1, n):
        source = lax.rem(me + n - k, n)
        pltpu.make_async_remote_copy(
            src_ref=x_ref,
            dst_ref=out_ref.at[source],
            send_sem=send_sem.at[k],
            recv_sem=recv_sem.at[source],
            device_id=device_of(source),
            device_id_type=pl.DeviceIdType.MESH,
        ).wait_recv()
    for copy in sends:
        copy.wait_send()
    local.wait()


def gather(x, axes, collective_id):
    sizes = tuple(lax.axis_size(a) for a in axes)
    n = math.prod(sizes)
    out = pl.pallas_call(
        functools.partial(gather_kernel, axes, sizes),
        out_shape=jax.ShapeDtypeStruct((n,) + x.shape, x.dtype),
        in_specs=[pl.BlockSpec(memory_space=pl.ANY)],
        out_specs=pl.BlockSpec(memory_space=pl.ANY),
        scratch_shapes=[
            pltpu.SemaphoreType.DMA((n,)),
            pltpu.SemaphoreType.DMA((n,)),
            pltpu.SemaphoreType.DMA,
        ],
        compiler_params=pltpu.CompilerParams(collective_id=collective_id, has_side_effects=True),
    )(x)
    return out.reshape((n * x.shape[0],) + x.shape[1:])


def score_kernel(rows_ref, cents_ref, noise_ref, out_ref, acc_ref):
    scores = lax.dot_general(
        rows_ref[...], cents_ref[...], (((1,), (1,)), ((), ())), preferred_element_type=jnp.float32
    )
    perturbed = inverse_temp * scores + noise_ref[...]
    lanes = acc_ref.shape[1]
    folded = perturbed[:, :lanes]
    for k in range(1, perturbed.shape[1] // lanes):
        folded = jnp.maximum(folded, perturbed[:, k * lanes:(k + 1) * lanes])
    step = pl.program_id(1)

    @pl.when(step == 0)
    def _():
        acc_ref[...] = folded

    @pl.when(step > 0)
    def _():
        acc_ref[...] = jnp.maximum(acc_ref[...], folded)

    @pl.when(step == pl.num_programs(1) - 1)
    def _():
        out_ref[...] = jnp.max(acc_ref[...], axis=1, keepdims=True)


def score_max(rows, cents, noise):
    count, width = rows.shape
    tm = min(1024, count)
    tn = min(1024, cents.shape[0])
    out = pl.pallas_call(
        score_kernel,
        out_shape=jax.ShapeDtypeStruct((count, 1), jnp.float32),
        grid=(count // tm, cents.shape[0] // tn),
        in_specs=[
            pl.BlockSpec((tm, width), lambda i, j: (i, 0)),
            pl.BlockSpec((tn, width), lambda i, j: (j, 0)),
            pl.BlockSpec((tm, tn), lambda i, j: (i, j)),
        ],
        out_specs=pl.BlockSpec((tm, 1), lambda i, j: (i, 0)),
        scratch_shapes=[pltpu.VMEM((tm, 128), jnp.float32)],
        compiler_params=pltpu.CompilerParams(dimension_semantics=("parallel", "arbitrary")),
    )(rows, cents, noise)
    return out[:, 0]


def cluster_stats(members, valid):
    feature_dim = members.shape[1]
    widened = members.astype(jnp.float32)
    scale = lax.rsqrt(jnp.mean(widened * widened, axis=1) + epsilon)
    gram = lax.dot_general(
        members, members, (((1,), (1,)), ((), ())), preferred_element_type=jnp.float32
    )
    similar = gram * scale[:, None] * scale[None, :] * (1.0 / math.sqrt(feature_dim))
    order = jnp.arange(members.shape[0], dtype=jnp.int32)
    usable = valid[None, :] & (order[:, None] != order[None, :])
    highest = jnp.max(jnp.where(usable, similar, -1e30), axis=1)
    scores = jnp.where(jnp.any(usable, axis=1), highest, 0.0)
    total = jnp.sum(jnp.where(valid[:, None], widened, 0.0), axis=0)
    center = total * lax.rsqrt(jnp.mean(total * total) + epsilon)
    return (scores, center)


def shards(embeddings, centroids, cluster, noise_salt):
    rows_dev, feature_dim = embeddings.shape
    cent_dev = centroids.shape[0]
    ny, nz, nx, nc = (lax.axis_size(a) for a in ALL)
    devices = ny * nz * nx * nc
    capacity = max(2, 2 * rows_dev // devices)
    iy, iz, ix, ic = (lax.axis_index(a) for a in ALL)
    me = ((iy * nz + iz) * nx + ix) * nc + ic
    salt_word = noise_salt[0]
    swap = [(i, (i + 1) % nc) for i in range(nc)]
    ring_y = [
        embeddings if s == 0 else lax.ppermute(embeddings, "y", [(i, (i + s) % ny) for i in range(ny)])
        for s in range(ny)
    ]
    group = jnp.concatenate(ring_y + [lax.ppermute(p, "c", swap) for p in ring_y], axis=0)
    piece = lax.all_gather(centroids, ("z", "x"), axis=0, tiled=True)
    src_c = jnp.stack([ic, (ic + nc - 1) % nc])
    src_y = (iy - jnp.arange(ny, dtype=jnp.int32)) % ny
    row_dev = ((src_y[None, :] * nz + iz) * nx + ix) * nc + src_c[:, None]
    group_ids = (row_dev[:, :, None] * rows_dev + jnp.arange(rows_dev, dtype=jnp.int32)).reshape(-1)
    cpos = jnp.arange(nz * nx * cent_dev, dtype=jnp.int32)
    cent_dev_ids = ((iy * nz + cpos // (nx * cent_dev)) * nx + cpos // cent_dev % nx) * nc + ic
    cent_ids = cent_dev_ids * cent_dev + cpos % cent_dev
    noise = gumbel_noise(group_ids[:, None], cent_ids[None, :], salt_word)
    result = score_max(group, piece, noise)
    owner = jnp.arange(ny * nc, dtype=jnp.int32)
    picked = (ic - owner % nc) % nc * ny + (iy - owner // nc) % ny
    outbound = jnp.take(result.reshape(nc * ny, rows_dev), picked, axis=0)
    inbound = lax.all_to_all(outbound, ("y", "c"), split_axis=0, concat_axis=0, tiled=True)
    perturbed_max = jnp.max(inbound, axis=0)
    assigned = cluster[:, 0]
    order = jnp.arange(rows_dev, dtype=jnp.int32)
    same = (assigned[:, None] == assigned[None, :]) & (order[None, :] < order[:, None])
    rank = jnp.sum(same.astype(jnp.int32), axis=1)
    slot = assigned * capacity + rank
    flag_width = 128
    tagged = jnp.concatenate([embeddings, jnp.ones((rows_dev, flag_width), jnp.bfloat16)], axis=1)
    outgoing = jnp.zeros((devices * capacity, feature_dim + flag_width), jnp.bfloat16).at[slot].set(tagged)
    received = lax.all_to_all(
        outgoing.reshape(devices, capacity, feature_dim + flag_width), ALL, split_axis=0, concat_axis=0, tiled=True
    ).reshape(devices * capacity, feature_dim + flag_width)
    members = received[:, :feature_dim]
    valid = received[:, feature_dim] > 0.5
    scores, center = cluster_stats(members, valid)
    returned = lax.all_to_all(
        scores.reshape(devices, capacity), ALL, split_axis=0, concat_axis=0, tiled=True
    )
    dedup_score = returned.reshape(devices * capacity)[slot]
    return (perturbed_max, dedup_score, center[None, :])


def solution(mesh):
    cent_count, rows_count = mesh.devices.shape
    cores = 2
    side = math.isqrt(rows_count // cores)
    view = Mesh(mesh.devices.reshape(cent_count, side, rows_count // cores // side, cores), ALL)
    spec = P(ALL, None)
    in_specs = (spec, spec, spec, P())
    out_specs = (P(ALL), P(ALL), spec)
    return jax.shard_map(shards, mesh=view, in_specs=in_specs, out_specs=out_specs, check_vma=False)
```

```python
import functools
import math

import jax
import jax.numpy as jnp
from jax import lax
from jax.experimental import pallas as pl
from jax.experimental.pallas import tpu as pltpu
from jax.sharding import Mesh
from jax.sharding import PartitionSpec as P

inverse_temp = 3.0
epsilon = 1e-06
ALL = ("y", "z", "x", "c")


def logical_shift(word, amount):
    return lax.shift_right_logical(word, jnp.full(word.shape, amount, jnp.int32))


def gumbel_noise(row_ids, cent_ids, salt_word):
    mixed = row_ids * 1103515245 + cent_ids * 739982445 + salt_word
    mixed = mixed ^ logical_shift(mixed, 16)
    mixed = mixed * 2146121005
    mixed = mixed ^ logical_shift(mixed, 15)
    mixed = mixed * 1759714725
    mixed = mixed ^ logical_shift(mixed, 16)
    low_bits = mixed & 8388607
    uniform = (low_bits.astype(jnp.float32) + 0.5) * (1.0 / 8388608.0)
    return -jnp.log(-jnp.log(uniform))


def gather_kernel(axes, sizes, x_ref, out_ref, send_sem, recv_sem, local_sem):
    n = math.prod(sizes)
    where = {a: lax.axis_index(a) for a in ALL}
    me = 0
    for a, size in zip(axes, sizes):
        me = me * size + where[a]

    def device_of(index):
        coords = dict(where)
        for a, size in reversed(list(zip(axes, sizes))):
            coords[a] = lax.rem(index, size)
            index = index // size
        return tuple(coords[a] for a in ALL)

    peers = [lax.rem(me + k, n) for k in range(n)]
    barrier = pltpu.get_barrier_semaphore()
    for k in range(1, n):
        pl.semaphore_signal(barrier, inc=1, device_id=device_of(peers[k]), device_id_type=pl.DeviceIdType.MESH)
    pl.semaphore_wait(barrier, n - 1)
    local = pltpu.make_async_copy(x_ref, out_ref.at[me], local_sem)
    local.start()
    sends = []
    for k in range(1, n):
        copy = pltpu.make_async_remote_copy(
            src_ref=x_ref,
            dst_ref=out_ref.at[me],
            send_sem=send_sem.at[k],
            recv_sem=recv_sem.at[me],
            device_id=device_of(peers[k]),
            device_id_type=pl.DeviceIdType.MESH,
        )
        copy.start()
        sends.append(copy)
    for k in range(1, n):
        source = lax.rem(me + n - k, n)
        pltpu.make_async_remote_copy(
            src_ref=x_ref,
            dst_ref=out_ref.at[source],
            send_sem=send_sem.at[k],
            recv_sem=recv_sem.at[source],
            device_id=device_of(source),
            device_id_type=pl.DeviceIdType.MESH,
        ).wait_recv()
    for copy in sends:
        copy.wait_send()
    local.wait()


def gather(x, axes, collective_id):
    sizes = tuple(lax.axis_size(a) for a in axes)
    n = math.prod(sizes)
    out = pl.pallas_call(
        functools.partial(gather_kernel, axes, sizes),
        out_shape=jax.ShapeDtypeStruct((n,) + x.shape, x.dtype),
        in_specs=[pl.BlockSpec(memory_space=pl.ANY)],
        out_specs=pl.BlockSpec(memory_space=pl.ANY),
        scratch_shapes=[
            pltpu.SemaphoreType.DMA((n,)),
            pltpu.SemaphoreType.DMA((n,)),
            pltpu.SemaphoreType.DMA,
        ],
        compiler_params=pltpu.CompilerParams(collective_id=collective_id, has_side_effects=True),
    )(x)
    return out.reshape((n * x.shape[0],) + x.shape[1:])


def score_kernel(rows_ref, cents_ref, noise_ref, out_ref, acc_ref):
    scores = lax.dot_general(
        rows_ref[...], cents_ref[...], (((1,), (1,)), ((), ())), preferred_element_type=jnp.float32
    )
    perturbed = inverse_temp * scores + noise_ref[...]
    lanes = acc_ref.shape[1]
    folded = perturbed[:, :lanes]
    for k in range(1, perturbed.shape[1] // lanes):
        folded = jnp.maximum(folded, perturbed[:, k * lanes:(k + 1) * lanes])
    step = pl.program_id(1)

    @pl.when(step == 0)
    def _():
        acc_ref[...] = folded

    @pl.when(step > 0)
    def _():
        acc_ref[...] = jnp.maximum(acc_ref[...], folded)

    @pl.when(step == pl.num_programs(1) - 1)
    def _():
        out_ref[...] = jnp.max(acc_ref[...], axis=1, keepdims=True)


def score_max(rows, cents, noise):
    count, width = rows.shape
    tm = min(2048, count)
    tn = min(512, cents.shape[0])
    out = pl.pallas_call(
        score_kernel,
        out_shape=jax.ShapeDtypeStruct((count, 1), jnp.float32),
        grid=(count // tm, cents.shape[0] // tn),
        in_specs=[
            pl.BlockSpec((tm, width), lambda i, j: (i, 0)),
            pl.BlockSpec((tn, width), lambda i, j: (j, 0)),
            pl.BlockSpec((tm, tn), lambda i, j: (i, j)),
        ],
        out_specs=pl.BlockSpec((tm, 1), lambda i, j: (i, 0)),
        scratch_shapes=[pltpu.VMEM((tm, 128), jnp.float32)],
        compiler_params=pltpu.CompilerParams(dimension_semantics=("parallel", "arbitrary")),
    )(rows, cents, noise)
    return out[:, 0]


def cluster_stats(members, valid):
    feature_dim = members.shape[1]
    widened = members.astype(jnp.float32)
    scale = lax.rsqrt(jnp.mean(widened * widened, axis=1) + epsilon)
    gram = lax.dot_general(
        members, members, (((1,), (1,)), ((), ())), preferred_element_type=jnp.float32
    )
    similar = gram * scale[:, None] * scale[None, :] * (1.0 / math.sqrt(feature_dim))
    order = jnp.arange(members.shape[0], dtype=jnp.int32)
    usable = valid[None, :] & (order[:, None] != order[None, :])
    highest = jnp.max(jnp.where(usable, similar, -1e30), axis=1)
    scores = jnp.where(jnp.any(usable, axis=1), highest, 0.0)
    total = jnp.sum(jnp.where(valid[:, None], widened, 0.0), axis=0)
    center = total * lax.rsqrt(jnp.mean(total * total) + epsilon)
    return (scores, center)


def shards(embeddings, centroids, cluster, noise_salt):
    rows_dev, feature_dim = embeddings.shape
    cent_dev = centroids.shape[0]
    ny, nz, nx, nc = (lax.axis_size(a) for a in ALL)
    devices = ny * nz * nx * nc
    capacity = max(2, 2 * rows_dev // devices)
    iy, iz, ix, ic = (lax.axis_index(a) for a in ALL)
    me = ((iy * nz + iz) * nx + ix) * nc + ic
    salt_word = noise_salt[0]
    swap = [(i, (i + 1) % nc) for i in range(nc)]
    ring_y = [
        embeddings if s == 0 else lax.ppermute(embeddings, "y", [(i, (i + s) % ny) for i in range(ny)])
        for s in range(ny)
    ]
    group = jnp.concatenate(ring_y + [lax.ppermute(p, "c", swap) for p in ring_y], axis=0)
    piece = lax.all_gather(centroids, ("z", "x"), axis=0, tiled=True)
    src_c = jnp.stack([ic, (ic + nc - 1) % nc])
    src_y = (iy - jnp.arange(ny, dtype=jnp.int32)) % ny
    row_dev = ((src_y[None, :] * nz + iz) * nx + ix) * nc + src_c[:, None]
    group_ids = (row_dev[:, :, None] * rows_dev + jnp.arange(rows_dev, dtype=jnp.int32)).reshape(-1)
    cpos = jnp.arange(nz * nx * cent_dev, dtype=jnp.int32)
    cent_dev_ids = ((iy * nz + cpos // (nx * cent_dev)) * nx + cpos // cent_dev % nx) * nc + ic
    cent_ids = cent_dev_ids * cent_dev + cpos % cent_dev
    noise = gumbel_noise(group_ids[:, None], cent_ids[None, :], salt_word)
    result = score_max(group, piece, noise)
    owner = jnp.arange(ny * nc, dtype=jnp.int32)
    picked = (ic - owner % nc) % nc * ny + (iy - owner // nc) % ny
    outbound = jnp.take(result.reshape(nc * ny, rows_dev), picked, axis=0)
    inbound = lax.all_to_all(outbound, ("y", "c"), split_axis=0, concat_axis=0, tiled=True)
    perturbed_max = jnp.max(inbound, axis=0)
    assigned = cluster[:, 0]
    order = jnp.arange(rows_dev, dtype=jnp.int32)
    same = (assigned[:, None] == assigned[None, :]) & (order[None, :] < order[:, None])
    rank = jnp.sum(same.astype(jnp.int32), axis=1)
    slot = assigned * capacity + rank
    flag_width = 128
    tagged = jnp.concatenate([embeddings, jnp.ones((rows_dev, flag_width), jnp.bfloat16)], axis=1)
    outgoing = jnp.zeros((devices * capacity, feature_dim + flag_width), jnp.bfloat16).at[slot].set(tagged)
    received = lax.all_to_all(
        outgoing.reshape(devices, capacity, feature_dim + flag_width), ALL, split_axis=0, concat_axis=0, tiled=True
    ).reshape(devices * capacity, feature_dim + flag_width)
    members = received[:, :feature_dim]
    valid = received[:, feature_dim] > 0.5
    scores, center = cluster_stats(members, valid)
    returned = lax.all_to_all(
        scores.reshape(devices, capacity), ALL, split_axis=0, concat_axis=0, tiled=True
    )
    dedup_score = returned.reshape(devices * capacity)[slot]
    return (perturbed_max, dedup_score, center[None, :])


def solution(mesh):
    cent_count, rows_count = mesh.devices.shape
    cores = 2
    side = math.isqrt(rows_count // cores)
    view = Mesh(mesh.devices.reshape(cent_count, side, rows_count // cores // side, cores), ALL)
    spec = P(ALL, None)
    in_specs = (spec, spec, spec, P())
    out_specs = (P(ALL), P(ALL), spec)
    return jax.shard_map(shards, mesh=view, in_specs=in_specs, out_specs=out_specs, check_vma=False)
```

```python
import functools
import math

import jax
import jax.numpy as jnp
from jax import lax
from jax.experimental import pallas as pl
from jax.experimental.pallas import tpu as pltpu
from jax.sharding import Mesh
from jax.sharding import PartitionSpec as P

inverse_temp = 3.0
epsilon = 1e-06
ALL = ("y", "z", "x", "c")


def logical_shift(word, amount):
    return lax.shift_right_logical(word, jnp.full(word.shape, amount, jnp.int32))


def gumbel_noise(row_ids, cent_ids, salt_word):
    mixed = row_ids * 1103515245 + cent_ids * 739982445 + salt_word
    mixed = mixed ^ logical_shift(mixed, 16)
    mixed = mixed * 2146121005
    mixed = mixed ^ logical_shift(mixed, 15)
    mixed = mixed * 1759714725
    mixed = mixed ^ logical_shift(mixed, 16)
    low_bits = mixed & 8388607
    uniform = (low_bits.astype(jnp.float32) + 0.5) * (1.0 / 8388608.0)
    return -jnp.log(-jnp.log(uniform))


def gather_kernel(axes, sizes, x_ref, out_ref, send_sem, recv_sem, local_sem):
    n = math.prod(sizes)
    where = {a: lax.axis_index(a) for a in ALL}
    me = 0
    for a, size in zip(axes, sizes):
        me = me * size + where[a]

    def device_of(index):
        coords = dict(where)
        for a, size in reversed(list(zip(axes, sizes))):
            coords[a] = lax.rem(index, size)
            index = index // size
        return tuple(coords[a] for a in ALL)

    peers = [lax.rem(me + k, n) for k in range(n)]
    barrier = pltpu.get_barrier_semaphore()
    for k in range(1, n):
        pl.semaphore_signal(barrier, inc=1, device_id=device_of(peers[k]), device_id_type=pl.DeviceIdType.MESH)
    pl.semaphore_wait(barrier, n - 1)
    local = pltpu.make_async_copy(x_ref, out_ref.at[me], local_sem)
    local.start()
    sends = []
    for k in range(1, n):
        copy = pltpu.make_async_remote_copy(
            src_ref=x_ref,
            dst_ref=out_ref.at[me],
            send_sem=send_sem.at[k],
            recv_sem=recv_sem.at[me],
            device_id=device_of(peers[k]),
            device_id_type=pl.DeviceIdType.MESH,
        )
        copy.start()
        sends.append(copy)
    for k in range(1, n):
        source = lax.rem(me + n - k, n)
        pltpu.make_async_remote_copy(
            src_ref=x_ref,
            dst_ref=out_ref.at[source],
            send_sem=send_sem.at[k],
            recv_sem=recv_sem.at[source],
            device_id=device_of(source),
            device_id_type=pl.DeviceIdType.MESH,
        ).wait_recv()
    for copy in sends:
        copy.wait_send()
    local.wait()


def gather(x, axes, collective_id):
    sizes = tuple(lax.axis_size(a) for a in axes)
    n = math.prod(sizes)
    out = pl.pallas_call(
        functools.partial(gather_kernel, axes, sizes),
        out_shape=jax.ShapeDtypeStruct((n,) + x.shape, x.dtype),
        in_specs=[pl.BlockSpec(memory_space=pl.ANY)],
        out_specs=pl.BlockSpec(memory_space=pl.ANY),
        scratch_shapes=[
            pltpu.SemaphoreType.DMA((n,)),
            pltpu.SemaphoreType.DMA((n,)),
            pltpu.SemaphoreType.DMA,
        ],
        compiler_params=pltpu.CompilerParams(collective_id=collective_id, has_side_effects=True),
    )(x)
    return out.reshape((n * x.shape[0],) + x.shape[1:])


def score_kernel(cents_ref, rows_ref, noise_ref, out_ref, acc_ref):
    scores = lax.dot_general(
        cents_ref[...], rows_ref[...], (((1,), (1,)), ((), ())), preferred_element_type=jnp.float32
    )
    perturbed = inverse_temp * scores + noise_ref[...]
    depth = acc_ref.shape[0]
    folded = jnp.max(perturbed.reshape(perturbed.shape[0] // depth, depth, perturbed.shape[1]), axis=0)
    step = pl.program_id(1)

    @pl.when(step == 0)
    def _():
        acc_ref[...] = folded

    @pl.when(step > 0)
    def _():
        acc_ref[...] = jnp.maximum(acc_ref[...], folded)

    @pl.when(step == pl.num_programs(1) - 1)
    def _():
        out_ref[...] = jnp.max(acc_ref[...], axis=0, keepdims=True)


def score_max(rows, cents, noise_t):
    count, width = rows.shape
    tm = min(1024, count)
    tn = min(1024, cents.shape[0])
    out = pl.pallas_call(
        score_kernel,
        out_shape=jax.ShapeDtypeStruct((1, count), jnp.float32),
        grid=(count // tm, cents.shape[0] // tn),
        in_specs=[
            pl.BlockSpec((tn, width), lambda i, j: (j, 0)),
            pl.BlockSpec((tm, width), lambda i, j: (i, 0)),
            pl.BlockSpec((tn, tm), lambda i, j: (j, i)),
        ],
        out_specs=pl.BlockSpec((1, tm), lambda i, j: (0, i)),
        scratch_shapes=[pltpu.VMEM((8, tm), jnp.float32)],
        compiler_params=pltpu.CompilerParams(dimension_semantics=("parallel", "arbitrary")),
    )(cents, rows, noise_t)
    return out[0]


def cluster_stats(members, valid):
    feature_dim = members.shape[1]
    widened = members.astype(jnp.float32)
    scale = lax.rsqrt(jnp.mean(widened * widened, axis=1) + epsilon)
    gram = lax.dot_general(
        members, members, (((1,), (1,)), ((), ())), preferred_element_type=jnp.float32
    )
    similar = gram * scale[:, None] * scale[None, :] * (1.0 / math.sqrt(feature_dim))
    order = jnp.arange(members.shape[0], dtype=jnp.int32)
    usable = valid[None, :] & (order[:, None] != order[None, :])
    highest = jnp.max(jnp.where(usable, similar, -1e30), axis=1)
    scores = jnp.where(jnp.any(usable, axis=1), highest, 0.0)
    total = jnp.sum(jnp.where(valid[:, None], widened, 0.0), axis=0)
    center = total * lax.rsqrt(jnp.mean(total * total) + epsilon)
    return (scores, center)


def shards(embeddings, centroids, cluster, noise_salt):
    rows_dev, feature_dim = embeddings.shape
    cent_dev = centroids.shape[0]
    ny, nz, nx, nc = (lax.axis_size(a) for a in ALL)
    devices = ny * nz * nx * nc
    capacity = max(2, 2 * rows_dev // devices)
    iy, iz, ix, ic = (lax.axis_index(a) for a in ALL)
    me = ((iy * nz + iz) * nx + ix) * nc + ic
    salt_word = noise_salt[0]
    swap = [(i, (i + 1) % nc) for i in range(nc)]
    ring_y = [
        embeddings if s == 0 else lax.ppermute(embeddings, "y", [(i, (i + s) % ny) for i in range(ny)])
        for s in range(ny)
    ]
    group = jnp.concatenate(ring_y + [lax.ppermute(p, "c", swap) for p in ring_y], axis=0)
    piece = lax.all_gather(centroids, ("z", "x"), axis=0, tiled=True)
    src_c = jnp.stack([ic, (ic + nc - 1) % nc])
    src_y = (iy - jnp.arange(ny, dtype=jnp.int32)) % ny
    row_dev = ((src_y[None, :] * nz + iz) * nx + ix) * nc + src_c[:, None]
    group_ids = (row_dev[:, :, None] * rows_dev + jnp.arange(rows_dev, dtype=jnp.int32)).reshape(-1)
    cpos = jnp.arange(nz * nx * cent_dev, dtype=jnp.int32)
    cent_dev_ids = ((iy * nz + cpos // (nx * cent_dev)) * nx + cpos // cent_dev % nx) * nc + ic
    cent_ids = cent_dev_ids * cent_dev + cpos % cent_dev
    noise_t = gumbel_noise(group_ids[None, :], cent_ids[:, None], salt_word)
    result = score_max(group, piece, noise_t)
    owner = jnp.arange(ny * nc, dtype=jnp.int32)
    picked = (ic - owner % nc) % nc * ny + (iy - owner // nc) % ny
    outbound = jnp.take(result.reshape(nc * ny, rows_dev), picked, axis=0)
    inbound = lax.all_to_all(outbound, ("y", "c"), split_axis=0, concat_axis=0, tiled=True)
    perturbed_max = jnp.max(inbound, axis=0)
    assigned = cluster[:, 0]
    order = jnp.arange(rows_dev, dtype=jnp.int32)
    same = (assigned[:, None] == assigned[None, :]) & (order[None, :] < order[:, None])
    rank = jnp.sum(same.astype(jnp.int32), axis=1)
    slot = assigned * capacity + rank
    flag_width = 128
    tagged = jnp.concatenate([embeddings, jnp.ones((rows_dev, flag_width), jnp.bfloat16)], axis=1)
    outgoing = jnp.zeros((devices * capacity, feature_dim + flag_width), jnp.bfloat16).at[slot].set(tagged)
    received = lax.all_to_all(
        outgoing.reshape(devices, capacity, feature_dim + flag_width), ALL, split_axis=0, concat_axis=0, tiled=True
    ).reshape(devices * capacity, feature_dim + flag_width)
    members = received[:, :feature_dim]
    valid = received[:, feature_dim] > 0.5
    scores, center = cluster_stats(members, valid)
    returned = lax.all_to_all(
        scores.reshape(devices, capacity), ALL, split_axis=0, concat_axis=0, tiled=True
    )
    dedup_score = returned.reshape(devices * capacity)[slot]
    return (perturbed_max, dedup_score, center[None, :])


def solution(mesh):
    cent_count, rows_count = mesh.devices.shape
    cores = 2
    side = math.isqrt(rows_count // cores)
    view = Mesh(mesh.devices.reshape(cent_count, side, rows_count // cores // side, cores), ALL)
    spec = P(ALL, None)
    in_specs = (spec, spec, spec, P())
    out_specs = (P(ALL), P(ALL), spec)
    return jax.shard_map(shards, mesh=view, in_specs=in_specs, out_specs=out_specs, check_vma=False)
```

```python
import functools
import math

import jax
import jax.numpy as jnp
from jax import lax
from jax.experimental import pallas as pl
from jax.experimental.pallas import tpu as pltpu
from jax.sharding import Mesh
from jax.sharding import PartitionSpec as P

inverse_temp = 3.0
epsilon = 1e-06
ALL = ("y", "z", "x", "c")


def logical_shift(word, amount):
    return lax.shift_right_logical(word, jnp.full(word.shape, amount, jnp.int32))


def gumbel_noise(row_ids, cent_ids, salt_word):
    mixed = row_ids * 1103515245 + cent_ids * 739982445 + salt_word
    mixed = mixed ^ logical_shift(mixed, 16)
    mixed = mixed * 2146121005
    mixed = mixed ^ logical_shift(mixed, 15)
    mixed = mixed * 1759714725
    mixed = mixed ^ logical_shift(mixed, 16)
    low_bits = mixed & 8388607
    uniform = (low_bits.astype(jnp.float32) + 0.5) * (1.0 / 8388608.0)
    return -jnp.log(-jnp.log(uniform))


def gather_kernel(axes, sizes, x_ref, out_ref, send_sem, recv_sem, local_sem):
    n = math.prod(sizes)
    where = {a: lax.axis_index(a) for a in ALL}
    me = 0
    for a, size in zip(axes, sizes):
        me = me * size + where[a]

    def device_of(index):
        coords = dict(where)
        for a, size in reversed(list(zip(axes, sizes))):
            coords[a] = lax.rem(index, size)
            index = index // size
        return tuple(coords[a] for a in ALL)

    peers = [lax.rem(me + k, n) for k in range(n)]
    barrier = pltpu.get_barrier_semaphore()
    for k in range(1, n):
        pl.semaphore_signal(barrier, inc=1, device_id=device_of(peers[k]), device_id_type=pl.DeviceIdType.MESH)
    pl.semaphore_wait(barrier, n - 1)
    local = pltpu.make_async_copy(x_ref, out_ref.at[me], local_sem)
    local.start()
    sends = []
    for k in range(1, n):
        copy = pltpu.make_async_remote_copy(
            src_ref=x_ref,
            dst_ref=out_ref.at[me],
            send_sem=send_sem.at[k],
            recv_sem=recv_sem.at[me],
            device_id=device_of(peers[k]),
            device_id_type=pl.DeviceIdType.MESH,
        )
        copy.start()
        sends.append(copy)
    for k in range(1, n):
        source = lax.rem(me + n - k, n)
        pltpu.make_async_remote_copy(
            src_ref=x_ref,
            dst_ref=out_ref.at[source],
            send_sem=send_sem.at[k],
            recv_sem=recv_sem.at[source],
            device_id=device_of(source),
            device_id_type=pl.DeviceIdType.MESH,
        ).wait_recv()
    for copy in sends:
        copy.wait_send()
    local.wait()


def gather(x, axes, collective_id):
    sizes = tuple(lax.axis_size(a) for a in axes)
    n = math.prod(sizes)
    out = pl.pallas_call(
        functools.partial(gather_kernel, axes, sizes),
        out_shape=jax.ShapeDtypeStruct((n,) + x.shape, x.dtype),
        in_specs=[pl.BlockSpec(memory_space=pl.ANY)],
        out_specs=pl.BlockSpec(memory_space=pl.ANY),
        scratch_shapes=[
            pltpu.SemaphoreType.DMA((n,)),
            pltpu.SemaphoreType.DMA((n,)),
            pltpu.SemaphoreType.DMA,
        ],
        compiler_params=pltpu.CompilerParams(collective_id=collective_id, has_side_effects=True),
    )(x)
    return out.reshape((n * x.shape[0],) + x.shape[1:])


def score_kernel(cents_ref, rows_ref, noise_ref, out_ref, acc_ref):
    scores = lax.dot_general(
        cents_ref[...], rows_ref[...], (((1,), (1,)), ((), ())), preferred_element_type=jnp.float32
    )
    perturbed = inverse_temp * scores + noise_ref[...]
    depth = acc_ref.shape[0]
    folded = jnp.max(perturbed.reshape(perturbed.shape[0] // depth, depth, perturbed.shape[1]), axis=0)
    step = pl.program_id(1)

    @pl.when(step == 0)
    def _():
        acc_ref[...] = folded

    @pl.when(step > 0)
    def _():
        acc_ref[...] = jnp.maximum(acc_ref[...], folded)

    @pl.when(step == pl.num_programs(1) - 1)
    def _():
        out_ref[...] = jnp.max(acc_ref[...], axis=0, keepdims=True)


def score_max(rows, cents, noise_t):
    count, width = rows.shape
    tm = min(1024, count)
    tn = min(1024, cents.shape[0])
    out = pl.pallas_call(
        score_kernel,
        out_shape=jax.ShapeDtypeStruct((1, count), jnp.float32),
        grid=(count // tm, cents.shape[0] // tn),
        in_specs=[
            pl.BlockSpec((tn, width), lambda i, j: (j, 0)),
            pl.BlockSpec((tm, width), lambda i, j: (i, 0)),
            pl.BlockSpec((tn, tm), lambda i, j: (j, i)),
        ],
        out_specs=pl.BlockSpec((1, tm), lambda i, j: (0, i)),
        scratch_shapes=[pltpu.VMEM((8, tm), jnp.float32)],
        compiler_params=pltpu.CompilerParams(dimension_semantics=("parallel", "arbitrary")),
    )(cents, rows, noise_t)
    return out[0]


def cluster_stats(members, valid):
    feature_dim = members.shape[1]
    widened = members.astype(jnp.float32)
    scale = lax.rsqrt(jnp.mean(widened * widened, axis=1) + epsilon)
    gram = lax.dot_general(
        members, members, (((1,), (1,)), ((), ())), preferred_element_type=jnp.float32
    )
    similar = gram * scale[:, None] * scale[None, :] * (1.0 / math.sqrt(feature_dim))
    order = jnp.arange(members.shape[0], dtype=jnp.int32)
    usable = valid[None, :] & (order[:, None] != order[None, :])
    highest = jnp.max(jnp.where(usable, similar, -1e30), axis=1)
    scores = jnp.where(jnp.any(usable, axis=1), highest, 0.0)
    total = jnp.sum(jnp.where(valid[:, None], widened, 0.0), axis=0)
    center = total * lax.rsqrt(jnp.mean(total * total) + epsilon)
    return (scores, center)


def shards(embeddings, centroids, cluster, noise_salt):
    rows_dev, feature_dim = embeddings.shape
    cent_dev = centroids.shape[0]
    ny, nz, nx, nc = (lax.axis_size(a) for a in ALL)
    devices = ny * nz * nx * nc
    capacity = max(2, 2 * rows_dev // devices)
    iy, iz, ix, ic = (lax.axis_index(a) for a in ALL)
    me = ((iy * nz + iz) * nx + ix) * nc + ic
    salt_word = noise_salt[0]
    swap = [(i, (i + 1) % nc) for i in range(nc)]
    ring_y = [
        embeddings if s == 0 else lax.ppermute(embeddings, "y", [(i, (i + s) % ny) for i in range(ny)])
        for s in range(ny)
    ]
    group = jnp.concatenate(ring_y + [lax.ppermute(p, "c", swap) for p in ring_y], axis=0)
    piece = lax.all_gather(centroids, ("z", "x"), axis=0, tiled=True)
    src_c = jnp.stack([ic, (ic + nc - 1) % nc])
    src_y = (iy - jnp.arange(ny, dtype=jnp.int32)) % ny
    row_dev = ((src_y[None, :] * nz + iz) * nx + ix) * nc + src_c[:, None]
    group_ids = (row_dev[:, :, None] * rows_dev + jnp.arange(rows_dev, dtype=jnp.int32)).reshape(-1)
    cpos = jnp.arange(nz * nx * cent_dev, dtype=jnp.int32)
    cent_dev_ids = ((iy * nz + cpos // (nx * cent_dev)) * nx + cpos // cent_dev % nx) * nc + ic
    cent_ids = cent_dev_ids * cent_dev + cpos % cent_dev
    noise_t = gumbel_noise(group_ids[None, :], cent_ids[:, None], salt_word)
    result = score_max(group, piece, noise_t)
    owner = jnp.arange(ny * nc, dtype=jnp.int32)
    picked = (ic - owner % nc) % nc * ny + (iy - owner // nc) % ny
    outbound = jnp.take(result.reshape(nc * ny, rows_dev), picked, axis=0)
    inbound = lax.all_to_all(outbound, ("y", "c"), split_axis=0, concat_axis=0, tiled=True)
    perturbed_max = jnp.max(inbound, axis=0)
    assigned = cluster[:, 0]
    order = jnp.arange(rows_dev, dtype=jnp.int32)
    same = (assigned[:, None] == assigned[None, :]) & (order[None, :] < order[:, None])
    rank = jnp.sum(same.astype(jnp.int32), axis=1)
    slot = assigned * capacity + rank
    flag_width = 128
    tagged = jnp.concatenate([embeddings, jnp.ones((rows_dev, flag_width), jnp.bfloat16)], axis=1)
    outgoing = jnp.zeros((devices * capacity, feature_dim + flag_width), jnp.bfloat16).at[slot].set(tagged)
    received = lax.all_to_all(
        outgoing.reshape(devices, capacity, feature_dim + flag_width), ALL, split_axis=0, concat_axis=0, tiled=True
    ).reshape(devices * capacity, feature_dim + flag_width)
    members = received[:, :feature_dim]
    valid = received[:, feature_dim] > 0.5
    scores, center = cluster_stats(members, valid)
    returned = lax.all_to_all(
        scores.reshape(devices, capacity), ALL, split_axis=0, concat_axis=0, tiled=True
    )
    back = returned.reshape(devices, capacity)
    hit = assigned[:, None] == jnp.arange(devices, dtype=jnp.int32)[None, :]
    by_owner = jnp.sum(jnp.where(hit[:, :, None], back[None, :, :], 0.0), axis=1)
    by_rank = rank[:, None] == jnp.arange(capacity, dtype=jnp.int32)[None, :]
    dedup_score = jnp.sum(jnp.where(by_rank, by_owner, 0.0), axis=1)
    return (perturbed_max, dedup_score, center[None, :])


def solution(mesh):
    cent_count, rows_count = mesh.devices.shape
    cores = 2
    side = math.isqrt(rows_count // cores)
    view = Mesh(mesh.devices.reshape(cent_count, side, rows_count // cores // side, cores), ALL)
    spec = P(ALL, None)
    in_specs = (spec, spec, spec, P())
    out_specs = (P(ALL), P(ALL), spec)
    return jax.shard_map(shards, mesh=view, in_specs=in_specs, out_specs=out_specs, check_vma=False)
```
